512 devices in a mesh: dp: 32 (over x, y, core), fsdp: 16 (over z).
Axes of the slice: x: 4, y: 4, z: 16, core: 2. Of those that a mesh axis runs over, the one named last changes fastest.
Arguments:
- acts: bfloat16 [65536, 4096], P(('dp', 'fsdp')), may hold values from -24 to 24
- cotangent: bfloat16 [65536, 512], P(('dp', 'fsdp')), may hold values from -6 to 6
- tenant: int32 [65536], P(('dp', 'fsdp')), may hold values from 0 to 255, as said below
- advantage: int32 [65536], P(('dp', 'fsdp')), may hold values from -8 to 8
- base_weight: bfloat16 [4096, 512], P('fsdp'), may hold values from -0.25 to 0.25
- a_param: float32 [4096, 8192], P('fsdp', 'dp'), may hold values from -6 to 6
- a_moment: float32 [4096, 8192], P('fsdp', 'dp'), may hold values from -6 to 6
- a_second: float32 [4096, 8192], P('fsdp', 'dp'), may hold values from 0.1 to 10
- b_param: float32 [8192, 512], P(('dp', 'fsdp')), may hold values from -6 to 6
- b_moment: float32 [8192, 512], P(('dp', 'fsdp')), may hold values from -6 to 6
- b_second: float32 [8192, 512], P(('dp', 'fsdp')), may hold values from 0.1 to 10
Outputs:
- grad_input: bfloat16 [65536, 4096], P(('dp', 'fsdp'))
- new_a_param: float32 [4096, 8192], P('fsdp', 'dp')
- new_a_moment: float32 [4096, 8192], P('fsdp', 'dp')
- new_a_second: float32 [4096, 8192], P('fsdp', 'dp')
- new_b_param: float32 [8192, 512], P(('dp', 'fsdp'))
- new_b_moment: float32 [8192, 512], P(('dp', 'fsdp'))
- new_b_second: float32 [8192, 512], P(('dp', 'fsdp'))
The draws below stay inside these ranges and needn't reach their ends.
Inputs may be any that keep to these rules, and one draw needn't show every extreme that they name: `tenant`: tenant t belongs to owner group t // 8. Among the 128 rows of each device, at most 9 belong to the tenants of one owner group; in every draw one owner group has exactly 9 rows on every device.
All inputs are finite; a program needn't handle non-finite values.
Results may differ from the reference program's by a relative error of at most 0.014.
Values may be sent and summed in bfloat16 or wider, within the bound.
A program may use at most 64 MiB of HBM per device.

```python
import math
import jax
import jax.numpy as jnp
from jax import lax

MODEL_WIDTH = 4096
KEY_FEATURES = 512
ADAPTER_RANK = 32
TEN_DEV = 8
RD = 128
OWNERS = 32
TENANTS = 256
CAP = 9
ROWS = 65536


def draw_tenant(key, part):
    groups = ROWS // RD
    base_key = jax.random.fold_in(key, 11)
    busy_owner = jax.random.randint(jax.random.fold_in(base_key, 1), (), 0, OWNERS)
    dev_keys = jax.random.split(jax.random.fold_in(base_key, 2), groups)
    position = jnp.arange(RD, dtype=jnp.int32)
    rank_of = jnp.where(position < CAP, 0, jnp.where(position < 2 * CAP, 1, 2 + (position - 2 * CAP) % (OWNERS - 2)))

    def one_device(subkey):
        first_key, second_key, third_key = jax.random.split(subkey, 3)
        scores = jax.random.permutation(first_key, OWNERS).astype(jnp.int32)
        scores = jnp.where(jnp.arange(OWNERS, dtype=jnp.int32) == busy_owner, -1, scores)
        ordered = jnp.argsort(scores).astype(jnp.int32)
        owner_rows = ordered[rank_of]
        local_id = jax.random.randint(second_key, (RD,), 0, TEN_DEV)
        labels = owner_rows * TEN_DEV + local_id
        shuffle = jax.random.permutation(third_key, RD)
        return labels[shuffle]
    return jax.vmap(one_device)(dev_keys).reshape(ROWS).astype(jnp.int32)


def touch_ends(drawn, key, least, top_value):
    longest = drawn.shape.index(max(drawn.shape))
    spots = []
    for shift in (0, 1):
        where = [jax.random.randint(jax.random.fold_in(key, axis), (), 0, length) for axis, length in enumerate(drawn.shape)]
        where[longest] = (where[longest] + shift) % drawn.shape[longest]
        spots.append(tuple(where))
    return drawn.at[spots[0]].set(least).at[spots[1]].set(top_value)


def strengthened(entries, key, source, target, blocks, factor):
    owner, partner = [(jnp.arange(entries.shape[dim]) // (entries.shape[dim] // blocks)).reshape([-1 if axis == dim else 1 for axis in range(entries.ndim)]) for dim in (source, target)]
    chosen = jax.random.permutation(key, blocks)[partner]
    strong = (owner == chosen) | (owner == (partner + blocks // 2) % blocks)
    return jnp.where(strong, factor * entries, entries)


def levels(key, extent, shards, smallest, high):
    def one(dim, shards_of):
        heights = jax.random.uniform(jax.random.fold_in(jax.random.fold_in(key, 6), dim), (shards_of,), jnp.float32, smallest / len(shards), high / len(shards))
        return jnp.repeat(jnp.exp(heights), extent[dim] // shards_of).reshape((-1,) + (1,) * (len(extent) - dim - 1))

    loudness = one(*shards[0])
    for cut in shards[1:]:
        loudness = loudness * one(*cut)
    return loudness


def noise(key, extent, spread, most, cuts=(), held_as=jnp.bfloat16):
    values = spread * jax.random.normal(key, extent, jnp.float32)
    if cuts:
        values = values * levels(key, extent, cuts, -0.22, 0.18)
    return jnp.clip(values, -most, most).astype(held_as)


def heavy_noise(own_key, shape, deviation, limit, shards, heavy, kind=jnp.bfloat16):
    array = deviation * jax.random.normal(own_key, shape, jnp.float32)
    if shards:
        array = array * levels(own_key, shape, shards, -0.22, 0.18)
    return jnp.clip(strengthened(array, jax.random.fold_in(own_key, 3), *heavy), -limit, limit).astype(kind)


def setup_inputs(seed: int = 0) -> dict:
    key_of = jax.random.split(jax.random.key(seed), 12)
    acts = heavy_noise(key_of[0], (ROWS, MODEL_WIDTH), 1.0, 24.0, ((0, 512),), (0, 1, 512, 6.0))
    cotangent = noise(key_of[1], (ROWS, KEY_FEATURES), 1.0, 6.0, ((0, 512),))
    tenant = draw_tenant(jax.random.fold_in(key_of[11], 71), 0)
    advantage = touch_ends(jax.random.randint(key_of[3], (ROWS,), -8, 9), jax.random.fold_in(key_of[3], 1), -8, 8).astype(jnp.int32)
    base_weight = noise(key_of[4], (MODEL_WIDTH, KEY_FEATURES), KEY_FEATURES ** -0.5, 0.25, ((0, 16),))
    a_param = noise(key_of[5], (MODEL_WIDTH, TENANTS * ADAPTER_RANK), 1.0, 6.0, ((0, 16), (1, 32)), jnp.float32)
    a_moment = noise(key_of[6], (MODEL_WIDTH, TENANTS * ADAPTER_RANK), 1.0, 6.0, ((0, 16), (1, 32)), jnp.float32)
    a_second = jnp.clip(jnp.exp(math.log(10.0) - 4.6051702 * jax.random.uniform(key_of[7], (MODEL_WIDTH, TENANTS * ADAPTER_RANK), jnp.float32) ** levels(key_of[7], (MODEL_WIDTH, TENANTS * ADAPTER_RANK), ((0, 16), (1, 32)), -0.2, 0.2)), 0.1, 10.0)
    b_param = noise(key_of[8], (TENANTS * ADAPTER_RANK, KEY_FEATURES), 1.0, 6.0, ((0, 512),), jnp.float32)
    b_moment = noise(key_of[9], (TENANTS * ADAPTER_RANK, KEY_FEATURES), 1.0, 6.0, ((0, 512),), jnp.float32)
    b_second = jnp.clip(jnp.exp(math.log(10.0) - 4.6051702 * jax.random.uniform(key_of[10], (TENANTS * ADAPTER_RANK, KEY_FEATURES), jnp.float32) ** levels(key_of[10], (TENANTS * ADAPTER_RANK, KEY_FEATURES), ((0, 512),), -0.2, 0.2)), 0.1, 10.0)
    return dict(acts=acts, cotangent=cotangent, tenant=tenant, advantage=advantage, base_weight=base_weight, a_param=a_param, a_moment=a_moment, a_second=a_second, b_param=b_param, b_moment=b_moment, b_second=b_second)


adapter_scale = 2.0
learn_rate = 0.02
beta_one = 0.9
beta_two = 0.999
adam_eps = 1e-08
bias_one = 1.0 - 0.9 ** 10
bias_two = 1.0 - 0.999 ** 10

def adam_step(param, moment, second, gradient):
    moment = beta_one * moment + (1.0 - beta_one) * gradient
    second = beta_two * second + (1.0 - beta_two) * gradient * gradient
    param = param - learn_rate * (moment / bias_one) / (jnp.sqrt(second / bias_two) + adam_eps)
    return (param, moment, second)

def reference(acts, cotangent, tenant, advantage, base_weight, a_param, a_moment, a_second, b_param, b_moment, b_second):
    tenant_index = TEN_DEV * OWNERS
    scaled = (cotangent.astype(jnp.float32) * (advantage.astype(jnp.float32) * 0.25)[:, None]).astype(jnp.bfloat16)
    a_low = (a_param * MODEL_WIDTH ** (-0.5)).astype(jnp.bfloat16)
    b_low = (b_param * ADAPTER_RANK ** (-0.5)).astype(jnp.bfloat16)
    a_stack = a_low.reshape(MODEL_WIDTH, tenant_index, ADAPTER_RANK).transpose(1, 0, 2)
    b_stack = b_low.reshape(tenant_index, ADAPTER_RANK, KEY_FEATURES)
    blocks = ROWS // RD
    acts_blocks = acts.reshape(blocks, RD, MODEL_WIDTH)
    scaled_blocks = scaled.reshape(blocks, RD, KEY_FEATURES)
    tenant_blocks = tenant.reshape(blocks, RD)

    def one_block(carry, inputs):
        down_gradient_total, up_gradient_total = carry
        x_blk, s_blk, t_blk = inputs
        down_factor_rows = a_stack[t_blk].astype(jnp.float32)
        b_rows = b_stack[t_blk].astype(jnp.float32)
        x_float = x_blk.astype(jnp.float32)
        s_float = s_blk.astype(jnp.float32)
        mid_proj = jnp.einsum('nd,ndr->nr', x_float, down_factor_rows).astype(jnp.bfloat16)
        backward_projection = jnp.einsum('nk,nrk->nr', s_float, b_rows).astype(jnp.bfloat16)
        adapter_branch_term = (adapter_scale * jnp.einsum('wt,wht->wh', backward_projection.astype(jnp.float32), down_factor_rows)).astype(jnp.bfloat16)
        base_term = jnp.dot(s_blk, base_weight.T, preferred_element_type=jnp.float32).astype(jnp.bfloat16)
        out_rows = (base_term.astype(jnp.float32) + adapter_branch_term.astype(jnp.float32)).astype(jnp.bfloat16)
        down_gradient_total = down_gradient_total.at[t_blk].add(x_float[:, :, None] * backward_projection.astype(jnp.float32)[:, None, :])
        up_gradient_total = up_gradient_total.at[t_blk].add(mid_proj.astype(jnp.float32)[:, :, None] * s_float[:, None, :])
        return ((down_gradient_total, up_gradient_total), out_rows)
    start = (jnp.zeros((tenant_index, MODEL_WIDTH, ADAPTER_RANK), jnp.float32), jnp.zeros((tenant_index, ADAPTER_RANK, KEY_FEATURES), jnp.float32))
    (down_gradient_total, up_gradient_total), out_blocks = lax.scan(one_block, start, (acts_blocks, scaled_blocks, tenant_blocks))
    grad_input = out_blocks.reshape(ROWS, MODEL_WIDTH)
    down_factor_gradient = (down_gradient_total * (adapter_scale * MODEL_WIDTH ** (-0.5))).transpose(1, 0, 2).reshape(MODEL_WIDTH, tenant_index * ADAPTER_RANK)
    up_factor_gradient = (up_gradient_total * (adapter_scale * ADAPTER_RANK ** (-0.5))).reshape(tenant_index * ADAPTER_RANK, KEY_FEATURES)
    new_a = adam_step(a_param, a_moment, a_second, down_factor_gradient)
    new_b = adam_step(b_param, b_moment, b_second, up_factor_gradient)
    return (grad_input, new_a[0], new_a[1], new_a[2], new_b[0], new_b[1], new_b[2])
```

```python
import functools

import jax
import jax.numpy as jnp
from jax import lax
from jax.experimental import pallas as pl
from jax.experimental.pallas import tpu as pltpu
from jax.sharding import PartitionSpec as P

MODEL_WIDTH = 4096
ADAPTER_RANK = 32
TEN_DEV = 8
MESH = pl.DeviceIdType.MESH

adapter_scale = 2.0
learn_rate = 0.02
beta_one = 0.9
beta_two = 0.999
adam_eps = 1e-08
bias_one = 1.0 - 0.9**10
bias_two = 1.0 - 0.999**10

ND = 32
NZ = 16
D = MODEL_WIDTH
KF = 512
RD = 128
CB = TEN_DEV * ADAPTER_RANK
SB = 8
MR = ND * SB
AR = MR + ND
PC = 8
PW = D // PC
DB = D // NZ
BB = CB // NZ
NCH = 4
CW = D // NCH
SMW = KF + 256

bf16 = jnp.bfloat16
f32 = jnp.float32


def dot_nn(a, b):
    return lax.dot_general(a, b, (((1,), (0,)), ((), ())), preferred_element_type=f32)


def dot_nt(a, b):
    return lax.dot_general(a, b, (((1,), (1,)), ((), ())), preferred_element_type=f32)


def one_hot(cond):
    return jnp.where(cond, 1.0, 0.0).astype(bf16)


def iota(shape, dim):
    return lax.broadcasted_iota(jnp.int32, shape, dim)


def exchange_kernel(
    tenant_ref,
    adv_ref,
    acts_hbm,
    cot_hbm,
    w_hbm,
    ap_hbm,
    bp_hbm,
    gi_ref,
    ga_ref,
    gb_ref,
    xb,
    cot,
    ap,
    bp,
    sx,
    sxe,
    ssm,
    rx,
    rxe,
    rsm,
    rs_all,
    scaled,
    a_all,
    b_all,
    w_all,
    back_s,
    back_t,
    mid_s,
    gbp,
    part,
    sd,
    se,
    rd,
    rde,
    sh,
    ls_send,
    ls_recv,
    gs_send,
    gs_recv,
    loc_sem,
    a2a_ss,
    a2a_rs,
    ag_ss,
    ag_rs,
    bg_ss,
    bg_rs,
    wg_ss,
    wg_rs,
    wx_ss,
    wx_rs,
    rs_ss,
    rs_rs,
    gr_ss,
    gr_rs,
):
    me = lax.axis_index("dp")
    z = lax.axis_index("fsdp")
    core = lax.rem(me, 2)
    mate = me + 1 - 2 * core
    right = lax.rem(z + 1, NZ)
    left = lax.rem(z + NZ - 1, NZ)
    zside = (right, left)

    loads = [
        pltpu.make_async_copy(src, dst, loc_sem.at[i])
        for i, (src, dst) in enumerate(
            [
                (bp_hbm, bp),
                (ap_hbm, ap),
                (cot_hbm, cot),
                (acts_hbm, xb),
                (w_hbm, w_all.at[pl.ds(pl.multiple_of(z * DB, DB), DB), :]),
            ]
        )
    ]
    for load in loads:
        load.start()
    barrier = pltpu.get_barrier_semaphore()

    def greet(k, carry):
        pl.semaphore_signal(
            barrier, inc=1, device_id=(lax.rem(me + k, ND), z), device_id_type=MESH
        )
        return carry

    lax.fori_loop(1, ND, greet, 0)
    for side in zside:
        pl.semaphore_signal(barrier, inc=1, device_id=(me, side), device_id_type=MESH)

    t_row = tenant_ref[...]
    t_col = jnp.broadcast_to(t_row.astype(f32), (RD, RD)).T.astype(jnp.int32)
    adv_col = jnp.broadcast_to(adv_ref[...].astype(f32), (RD, RD)).T[:, 0:1]
    o_row = jnp.right_shift(t_row, 3)
    o_col = jnp.right_shift(t_col, 3)
    tl = jnp.bitwise_and(t_col, TEN_DEV - 1).astype(f32).astype(bf16)
    same = o_col == o_row
    earlier_rows = jnp.where(same & (iota((RD, RD), 0) < iota((RD, RD), 1)), 1.0, 0.0)
    rank_row = jnp.sum(earlier_rows, axis=0, keepdims=True).astype(jnp.int32)
    earlier_cols = jnp.where(same & (iota((RD, RD), 1) < iota((RD, RD), 0)), 1.0, 0.0)
    rank_col = jnp.sum(earlier_cols, axis=1, keepdims=True).astype(jnp.int32)
    key8_row = jnp.where(rank_row < SB, o_row * SB + rank_row, -1)
    key9_row = jnp.where(rank_row == SB, o_row, -1)
    o_col1 = o_col[:, 0:1]
    key8_col = jnp.where(rank_col < SB, o_col1 * SB + rank_col, -1)
    key9_col = jnp.where(rank_col == SB, o_col1, -1)
    p8 = one_hot(iota((MR, RD), 0) == key8_row)
    ext_rows = jnp.right_shift(iota((MR, RD), 0), 3) == key9_row
    ext_piece = jnp.bitwise_and(iota((MR, RD), 0), PC - 1)

    def pack9(p):
        return one_hot(ext_rows & (ext_piece == p))

    loads[0].wait()
    b_all[pl.ds(pl.multiple_of(z * BB, BB), BB), :] = (
        bp[...] * ADAPTER_RANK ** (-0.5)
    ).astype(bf16)
    loads[1].wait()
    a_all[pl.ds(pl.multiple_of(z * DB, DB), DB), :] = (
        ap[...] * MODEL_WIDTH ** (-0.5)
    ).astype(bf16)

    loads[2].wait()
    scaled_rows = (cot[...].astype(f32) * (adv_col * 0.25)).astype(bf16)
    scaled[...] = scaled_rows
    ssm[:, 0:KF] = dot_nn(p8, scaled_rows).astype(bf16)
    ssm[:, KF : KF + 128] = dot_nn(p8, tl).astype(bf16)
    misc = jnp.zeros((MR, 128), f32)
    for p in range(PC):
        part9 = scaled_rows[:, 128 * p : 128 * p + 128] if p < 4 else tl
        misc = misc + dot_nn(pack9(p), part9)
    ssm[:, KF + 128 : KF + 256] = misc.astype(bf16)

    pl.semaphore_wait(barrier, ND - 1 + 2)

    def a2a_start(src, dst, c0, cw, i):
        def go(k, carry):
            peer = lax.rem(me + k, ND)
            pltpu.make_async_remote_copy(
                src_ref=src.at[pl.ds(pl.multiple_of(peer * SB, SB), SB), pl.ds(c0, cw)],
                dst_ref=dst.at[pl.ds(pl.multiple_of(me * SB, SB), SB), pl.ds(c0, cw)],
                send_sem=a2a_ss.at[i],
                recv_sem=a2a_rs.at[i],
                device_id=(peer, z),
                device_id_type=MESH,
            ).start()
            return carry

        lax.fori_loop(1, ND, go, 0)
        own = pl.ds(pl.multiple_of(me * SB, SB), SB)
        dst[own, c0 : c0 + cw] = src[own, c0 : c0 + cw]

    def a2a_all(src, dst, c0, cw, i):
        return pltpu.make_async_remote_copy(
            src_ref=src.at[pl.ds(0, MR - SB), pl.ds(c0, cw)],
            dst_ref=dst.at[pl.ds(0, MR - SB), pl.ds(c0, cw)],
            send_sem=a2a_ss.at[i],
            recv_sem=a2a_rs.at[i],
            device_id=(mate, z),
            device_id_type=MESH,
        )

    def gather_copy(buf, ss, rs, rows, off, size, dr, step):
        block = lax.rem(z - step + NZ, NZ) if dr == 0 else lax.rem(z + step, NZ)
        view = buf.at[pl.ds(pl.multiple_of(block * rows + off, size), size), :]
        return pltpu.make_async_remote_copy(
            src_ref=view,
            dst_ref=view,
            send_sem=ss,
            recv_sem=rs,
            device_id=(me, zside[dr]),
            device_id_type=MESH,
        )

    steps = (NZ // 2, NZ // 2 - 1)
    HB = DB // 2

    def a_copy(dr, s, q):
        return gather_copy(
            a_all, ag_ss.at[dr, s, q], ag_rs.at[dr, s, q], DB, q * HB, HB, dr, s
        )

    def b_copy(dr, s):
        return gather_copy(b_all, bg_ss.at[dr, s], bg_rs.at[dr, s], BB, 0, BB, dr, s)

    def w_copy(dr, s):
        block = lax.rem(z - s + NZ, NZ) if dr == 0 else lax.rem(z + s, NZ)
        view = w_all.at[pl.ds(pl.multiple_of(block * DB + core * HB, HB), HB), :]
        return pltpu.make_async_remote_copy(
            src_ref=view,
            dst_ref=view,
            send_sem=wg_ss.at[dr, s],
            recv_sem=wg_rs.at[dr, s],
            device_id=(me, zside[dr]),
            device_id_type=MESH,
        )

    def w_mate(dr, s):
        block = lax.rem(z - s - 1 + NZ, NZ) if dr == 0 else lax.rem(z + s + 1, NZ)
        view = w_all.at[pl.ds(pl.multiple_of(block * DB + core * HB, HB), HB), :]
        return pltpu.make_async_remote_copy(
            src_ref=view,
            dst_ref=view,
            send_sem=wx_ss.at[dr, s],
            recv_sem=wx_rs.at[dr, s],
            device_id=(mate, z),
            device_id_type=MESH,
        )

    def ab_step(s):
        for dr in (0, 1):
            if s > 0 and s - 1 < steps[dr]:
                b_copy(dr, s - 1).wait_recv()
            if s < steps[dr]:
                b_copy(dr, s).start()
        for q in (0, 1):
            for dr in (0, 1):
                if s > 0 and s - 1 < steps[dr]:
                    a_copy(dr, s - 1, q).wait_recv()
                if s < steps[dr]:
                    a_copy(dr, s, q).start()

    def w_step(s):
        for dr in (0, 1):
            if s > 0 and s - 1 < steps[dr]:
                w_copy(dr, s - 1).wait_recv()
            if s < steps[dr]:
                w_copy(dr, s).start()
            if s > 0 and s - 1 < steps[dr]:
                w_mate(dr, s - 1).start()

    def base_block(block):
        cols = pl.ds(pl.multiple_of(block * DB, DB), DB)
        rows = pl.ds(pl.multiple_of(block * DB, DB), DB)
        gi_ref[:, cols] = dot_nt(scaled[...], w_all[rows, :]).astype(bf16)

    def base_step(s):
        for dr in (0, 1):
            if s < steps[dr]:
                w_mate(dr, s).wait_recv()
                base_block(
                    lax.rem(z - s - 1 + NZ, NZ) if dr == 0 else lax.rem(z + s + 1, NZ)
                )

    ab_step(0)
    a2a_start(ssm, rsm, 0, SMW, 0)
    loads[3].wait()

    def pack_pieces(p, acc):
        cols = pl.ds(pl.multiple_of(p * PW, PW), PW)
        return acc + dot_nn(one_hot(ext_rows & (ext_piece == p)), xb[:, cols])

    for ch in range(NCH):
        for h in range(CW // 512):
            c0 = ch * CW + h * 512
            sx[:, c0 : c0 + 512] = dot_nn(p8, xb[:, c0 : c0 + 512]).astype(bf16)
        a2a_start(sx, rx, ch * CW, CW, 1 + ch)
        if ch == 0:
            sxe[...] = lax.fori_loop(0, PC, pack_pieces, jnp.zeros((MR, PW), f32)).astype(bf16)
            a2a_start(sxe, rxe, 0, PW, 1 + NCH)
            loads[4].wait()
        ab_step(ch + 1)
        if ch % 2 == 0:
            w_step(ch // 2)
    for s in range(NCH + 1, 8):
        ab_step(s)
        if s == 5:
            w_step(2)
        if s == 6:
            base_block(z)
            base_step(0)
        if s == 7:
            w_step(3)
            base_step(1)
    ab_step(8)

    def pick9(p):
        return one_hot(iota((ND, MR), 1) == iota((ND, MR), 0) * PC + p)

    a2a_all(ssm, rsm, 0, SMW, 0).wait_recv()
    rs_all[0:MR, :] = rsm[:, 0:KF]
    misc_in = rsm[:, KF + 128 : KF + 256]
    for p in range(4):
        rs_all[MR:AR, 128 * p : 128 * p + 128] = dot_nn(pick9(p), misc_in).astype(bf16)
    t_all = jnp.concatenate(
        [rsm[:, KF : KF + 128].astype(f32), dot_nn(pick9(4), misc_in)], axis=0
    ).astype(jnp.int32)
    mask = jnp.right_shift(iota((AR, CB), 1), 5) == jnp.concatenate([t_all, t_all], axis=1)
    back_f = jnp.where(mask, dot_nt(rs_all[...], b_all[...]), 0.0)
    back_s[...] = back_f.astype(bf16)
    back_t[...] = back_f.T.astype(bf16)

    for ch in range(NCH):
        a2a_all(sx, rx, ch * CW, CW, 1 + ch).wait_recv()
    a2a_all(sxe, rxe, 0, PW, 1 + NCH).wait_recv()
    for p in range(PC):
        rx[MR:AR, p * PW : p * PW + PW] = dot_nn(pick9(p), rxe[...]).astype(bf16)

    down_coefficient = adapter_scale * MODEL_WIDTH ** (-0.5)
    up_coefficient = adapter_scale * ADAPTER_RANK ** (-0.5)

    rsteps = (NZ // 2, NZ // 2 - 1)

    def target(dr, k):
        return lax.rem(z + NZ - 8 + k, NZ) if dr == 0 else lax.rem(z + 7 - k, NZ)

    def a_partial(block):
        cols = pl.ds(pl.multiple_of(block * DB, DB), DB)
        return down_coefficient * dot_nn(back_t[...], rx[:, cols])

    def rs_copy(dr, k, q):
        rows = pl.ds(q * HB, HB)
        return pltpu.make_async_remote_copy(
            src_ref=ls_send.at[dr, k, rows, :],
            dst_ref=ls_recv.at[dr, k, rows, :],
            send_sem=rs_ss.at[dr, k, q],
            recv_sem=rs_rs.at[dr, k, q],
            device_id=(me, (left, right)[dr]),
            device_id_type=MESH,
        )

    def gb_copy(dr, k):
        return pltpu.make_async_remote_copy(
            src_ref=gs_send.at[dr, k],
            dst_ref=gs_recv.at[dr, k],
            send_sem=gr_ss.at[dr, k],
            recv_sem=gr_rs.at[dr, k],
            device_id=(me, (left, right)[dr]),
            device_id_type=MESH,
        )

    def rs_parts(k):
        for dr in (0, 1):
            if k < rsteps[dr]:
                part[dr] = a_partial(target(dr, k))

    def rs_step(k):
        for q in (0, 1):
            rows = slice(q * HB, q * HB + HB)
            for dr in (0, 1):
                if k < rsteps[dr]:
                    total = part[dr, rows, :]
                    if k > 0:
                        rs_copy(dr, k - 1, q).wait_recv()
                        total = total + ls_recv[dr, k - 1, rows, :].astype(f32)
                    ls_send[dr, k, rows, :] = total.astype(bf16)
                    rs_copy(dr, k, q).start()

    def gb_rows(block):
        return gbp[pl.ds(pl.multiple_of(block * BB, BB), BB), :]

    def gb_step(k):
        for dr in (0, 1):
            if k < rsteps[dr]:
                total = gb_rows(target(dr, k))
                if k > 0:
                    gb_copy(dr, k - 1).wait_recv()
                    total = total + gs_recv[dr, k - 1].astype(f32)
                gs_send[dr, k] = total.astype(bf16)
                gb_copy(dr, k).start()

    def put9(p):
        return one_hot(iota((MR, ND), 0) == iota((MR, ND), 1) * PC + p)

    def side_chunk(ch, acc):
        for h in range(CW // PW):
            p = ch * (CW // PW) + h
            term = (
                adapter_scale * dot_nt(back_s[...], a_all[p * PW : p * PW + PW, :])
            ).astype(bf16)
            sd[:, p * PW : p * PW + PW] = term[0:MR]
            acc = acc + dot_nn(put9(p), term[MR:AR])
        a2a_start(sd, rd, ch * CW, CW, NCH + 2 + ch)
        return acc

    rs_parts(0)
    rs_step(0)
    ext = side_chunk(0, jnp.zeros((MR, PW), f32))
    mid = dot_nn(rx[...], a_all[...])
    mid_s[...] = jnp.where(mask, mid, 0.0).T.astype(bf16)
    gbp[...] = up_coefficient * dot_nn(mid_s[...], rs_all[...])
    gb_step(0)
    rs_parts(1)
    ext = side_chunk(1, ext)
    rs_step(1)
    ext = side_chunk(2, ext)
    ext = side_chunk(3, ext)
    se[...] = ext.astype(bf16)
    a2a_start(se, rde, 0, PW, 2 * NCH + 2)
    w_step(4)
    gb_step(1)
    base_step(2)
    for k in range(2, 8):
        rs_parts(k)
        rs_step(k)
        gb_step(k)
        if k % 2 == 0:
            w_step(k // 2 + 4)
            base_step(k // 2 + 2)
    r8 = one_hot(iota((RD, MR), 1) == key8_col)
    back_rows = jnp.right_shift(iota((RD, MR), 1), 3) == key9_col
    back_piece = jnp.bitwise_and(iota((RD, MR), 1), PC - 1)
    for ch in range(NCH):
        a2a_all(sd, rd, ch * CW, CW, NCH + 2 + ch).wait_recv()
    a2a_all(se, rde, 0, PW, 2 * NCH + 2).wait_recv()
    for p in range(PC):
        cols = slice(p * PW, p * PW + PW)
        r9 = one_hot(back_rows & (back_piece == p))
        sh[:, cols] = (dot_nn(r8, rd[:, cols]) + dot_nn(r9, rde[...])).astype(bf16)

    total = a_partial(z)
    for q in (0, 1):
        for dr in (0, 1):
            rs_copy(dr, rsteps[dr] - 1, q).wait_recv()
    total = total + ls_recv[0, rsteps[0] - 1].astype(f32)
    total = total + ls_recv[1, rsteps[1] - 1].astype(f32)
    ga_ref[...] = total.T
    for dr in (0, 1):
        gb_copy(dr, rsteps[dr] - 1).wait_recv()
    gb_ref[...] = (
        gb_rows(z)
        + gs_recv[0, rsteps[0] - 1].astype(f32)
        + gs_recv[1, rsteps[1] - 1].astype(f32)
    )
    w_step(8)
    base_step(6)
    base_step(7)
    for p in range(PC):
        cols = slice(p * PW, p * PW + PW)
        gi_ref[:, cols] = (gi_ref[:, cols].astype(f32) + sh[:, cols].astype(f32)).astype(bf16)

    a2a_all(ssm, rsm, 0, SMW, 0).wait_send()
    for ch in range(NCH):
        a2a_all(sx, rx, ch * CW, CW, 1 + ch).wait_send()
        a2a_all(sd, rd, ch * CW, CW, NCH + 2 + ch).wait_send()
    a2a_all(sxe, rxe, 0, PW, 1 + NCH).wait_send()
    a2a_all(se, rde, 0, PW, 2 * NCH + 2).wait_send()
    for dr in (0, 1):
        for s in range(steps[dr]):
            for q in (0, 1):
                a_copy(dr, s, q).wait_send()
            b_copy(dr, s).wait_send()
            w_copy(dr, s).wait_send()
            w_mate(dr, s).wait_send()
        for k in range(rsteps[dr]):
            for q in (0, 1):
                rs_copy(dr, k, q).wait_send()
            gb_copy(dr, k).wait_send()


def adam_refs(param, moment, second, gradient, out_param, out_moment, out_second):
    new_moment = beta_one * moment[...] + (1.0 - beta_one) * gradient
    new_second = beta_two * second[...] + (1.0 - beta_two) * gradient * gradient
    out_moment[...] = new_moment
    out_second[...] = new_second
    out_param[...] = param[...] - learn_rate * (new_moment / bias_one) / (
        jnp.sqrt(new_second / bias_two) + adam_eps
    )


def finish_kernel(
    gi, ga, gb, ap, am, av, bp, bm, bv, gi_out, ap_out, am_out, av_out, bp_out, bm_out, bv_out
):
    gi_out[...] = gi[...]
    adam_refs(ap, am, av, ga[...], ap_out, am_out, av_out)
    adam_refs(bp, bm, bv, gb[...], bp_out, bm_out, bv_out)


def per_device(
    acts,
    cotangent,
    tenant,
    advantage,
    base_weight,
    a_param,
    a_moment,
    a_second,
    b_param,
    b_moment,
    b_second,
):
    vmem = pl.BlockSpec(memory_space=pltpu.VMEM)
    hbm = pl.BlockSpec(memory_space=pl.ANY)
    dma = pltpu.SemaphoreType.DMA
    v = pltpu.VMEM
    gi, ga, gb = pl.pallas_call(
        exchange_kernel,
        out_shape=(
            jax.ShapeDtypeStruct((RD, D), bf16),
            jax.ShapeDtypeStruct((DB, CB), f32),
            jax.ShapeDtypeStruct((BB, KF), f32),
        ),
        in_specs=[vmem, vmem, hbm, hbm, hbm, hbm, hbm],
        out_specs=(vmem, vmem, vmem),
        scratch_shapes=[
            v((RD, D), bf16),
            v((RD, KF), bf16),
            v((DB, CB), f32),
            v((BB, KF), f32),
            v((MR, D), bf16),
            v((MR, PW), bf16),
            v((MR, SMW), bf16),
            v((AR, D), bf16),
            v((MR, PW), bf16),
            v((MR, SMW), bf16),
            v((AR, KF), bf16),
            v((RD, KF), bf16),
            v((D, CB), bf16),
            v((CB, KF), bf16),
            v((D, KF), bf16),
            v((AR, CB), bf16),
            v((CB, AR), bf16),
            v((CB, AR), bf16),
            v((CB, KF), f32),
            v((2, CB, DB), f32),
            v((MR, D), bf16),
            v((MR, PW), bf16),
            v((MR, D), bf16),
            v((MR, PW), bf16),
            v((RD, D), bf16),
            v((2, 8, CB, DB), bf16),
            v((2, 8, CB, DB), bf16),
            v((2, 8, BB, KF), bf16),
            v((2, 8, BB, KF), bf16),
            dma((5,)),
            dma((2 * NCH + 3,)),
            dma((2 * NCH + 3,)),
            dma((2, 8, 2)),
            dma((2, 8, 2)),
            dma((2, 8)),
            dma((2, 8)),
            dma((2, 8)),
            dma((2, 8)),
            dma((2, 8)),
            dma((2, 8)),
            dma((2, 8, 2)),
            dma((2, 8, 2)),
            dma((2, 8)),
            dma((2, 8)),
        ],
        compiler_params=pltpu.CompilerParams(
            collective_id=0, has_side_effects=True, vmem_limit_bytes=48 * 1024 * 1024
        ),
        name="exchange",
    )(
        tenant.reshape(1, RD),
        advantage.reshape(1, RD),
        acts,
        cotangent,
        base_weight,
        a_param,
        b_param,
    )
    return tuple(
        pl.pallas_call(
            finish_kernel,
            out_shape=(
                jax.ShapeDtypeStruct((RD, D), bf16),
                *[jax.ShapeDtypeStruct((DB, CB), f32)] * 3,
                *[jax.ShapeDtypeStruct((BB, KF), f32)] * 3,
            ),
            in_specs=[vmem] * 9,
            out_specs=(vmem,) * 7,
            name="finish",
        )(gi, ga, gb, a_param, a_moment, a_second, b_param, b_moment, b_second)
    )


def solution(mesh):
    in_specs = (
        P(("dp", "fsdp"), None),
        P(("dp", "fsdp"), None),
        P(("dp", "fsdp")),
        P(("dp", "fsdp")),
        P("fsdp", None),
        P("fsdp", "dp"),
        P("fsdp", "dp"),
        P("fsdp", "dp"),
        P(("dp", "fsdp"), None),
        P(("dp", "fsdp"), None),
        P(("dp", "fsdp"), None),
    )
    out_specs = (
        P(("dp", "fsdp"), None),
        P("fsdp", "dp"),
        P("fsdp", "dp"),
        P("fsdp", "dp"),
        P(("dp", "fsdp"), None),
        P(("dp", "fsdp"), None),
        P(("dp", "fsdp"), None),
    )
    return jax.shard_map(
        per_device, mesh=mesh, in_specs=in_specs, out_specs=out_specs, check_vma=False
    )
```

```python
import functools

import jax
import jax.numpy as jnp
from jax import lax
from jax.experimental import pallas as pl
from jax.experimental.pallas import tpu as pltpu
from jax.sharding import PartitionSpec as P

MODEL_WIDTH = 4096
ADAPTER_RANK = 32
TEN_DEV = 8
MESH = pl.DeviceIdType.MESH

adapter_scale = 2.0
learn_rate = 0.02
beta_one = 0.9
beta_two = 0.999
adam_eps = 1e-08
bias_one = 1.0 - 0.9**10
bias_two = 1.0 - 0.999**10

ND = 32
NZ = 16
D = MODEL_WIDTH
KF = 512
RD = 128
CB = TEN_DEV * ADAPTER_RANK
SB = 8
MR = ND * SB
AR = MR + ND
PC = 8
PW = D // PC
DB = D // NZ
BB = CB // NZ
NCH = 4
CW = D // NCH
SMW = KF + 256
WR = DB // 8
W_RANGES = ((1, 4), (12, 4), (5, 3), (8, 4))

bf16 = jnp.bfloat16
f32 = jnp.float32


def dot_nn(a, b):
    return lax.dot_general(a, b, (((1,), (0,)), ((), ())), preferred_element_type=f32)


def dot_nt(a, b):
    return lax.dot_general(a, b, (((1,), (1,)), ((), ())), preferred_element_type=f32)


def one_hot(cond):
    return jnp.where(cond, 1.0, 0.0).astype(bf16)


def iota(shape, dim):
    return lax.broadcasted_iota(jnp.int32, shape, dim)


def adam_refs(param, moment, second, gradient, out_param, out_moment, out_second):
    new_moment = beta_one * moment[...] + (1.0 - beta_one) * gradient
    new_second = beta_two * second[...] + (1.0 - beta_two) * gradient * gradient
    out_moment[...] = new_moment
    out_second[...] = new_second
    out_param[...] = param[...] - learn_rate * (new_moment / bias_one) / (
        jnp.sqrt(new_second / bias_two) + adam_eps
    )


def exchange_kernel(
    tenant_hbm,
    adv_hbm,
    acts_hbm,
    cot_hbm,
    w_hbm,
    ap_hbm,
    am_hbm,
    av_hbm,
    bp_hbm,
    bm_hbm,
    bv_hbm,
    gi_ref,
    ap_out,
    am_out,
    av_out,
    bp_out,
    bm_out,
    bv_out,
    tenant_ref,
    adv_ref,
    xb,
    cot,
    ap,
    am,
    av,
    bp,
    bm,
    bv,
    sx,
    sxe,
    ssm,
    rx,
    rxe,
    rsm,
    rs_all,
    scaled,
    a_all,
    b_all,
    w_all,
    back_s,
    back_t,
    mid_s,
    gbp,
    part,
    sd,
    se,
    rd,
    rde,
    ls_send,
    ls_recv,
    gs_send,
    gs_recv,
    loc_sem,
    a2a_ss,
    a2a_rs,
    ag_ss,
    ag_rs,
    bg_ss,
    bg_rs,
    wg_ss,
    wg_rs,
    wx_ss,
    wx_rs,
    wf_ss,
    wf_rs,
    rs_ss,
    rs_rs,
    gr_ss,
    gr_rs,
):
    me = lax.axis_index("dp")
    z = lax.axis_index("fsdp")
    core = lax.rem(me, 2)
    mate = me + 1 - 2 * core
    x = me // 8
    y = lax.rem(me // 2, 4)
    quarter = lax.rem(x + 2 * y, 4)

    def chip(cx, cy):
        return (lax.rem(cx, 4) * 4 + lax.rem(cy, 4)) * 2 + core

    near = (chip(x + 1, y), chip(x + 3, y), chip(x, y + 1), chip(x, y + 3))
    right = lax.rem(z + 1, NZ)
    left = lax.rem(z + NZ - 1, NZ)
    zside = (right, left)

    loads = [
        pltpu.make_async_copy(src, dst, loc_sem.at[i])
        for i, (src, dst) in enumerate(
            [
                (tenant_hbm, tenant_ref),
                (adv_hbm, adv_ref),
                (bp_hbm, bp),
                (ap_hbm, ap),
                (cot_hbm, cot),
                (acts_hbm, xb),
                (am_hbm, am),
                (av_hbm, av),
                (bm_hbm, bm),
                (bv_hbm, bv),
                *[
                    (
                        w_hbm.at[(2 * c + k) * WR : (2 * c + k + 1) * WR, :],
                        w_all.at[c, k, 0],
                    )
                    for c in range(4)
                    for k in range(2)
                ],
            ]
        )
    ]
    for load in loads:
        load.start()
    barrier = pltpu.get_barrier_semaphore()

    def greet(k, carry):
        pl.semaphore_signal(
            barrier, inc=1, device_id=(lax.rem(me + k, ND), z), device_id_type=MESH
        )
        return carry

    lax.fori_loop(1, ND, greet, 0)
    for side in zside:
        pl.semaphore_signal(barrier, inc=1, device_id=(me, side), device_id_type=MESH)

    loads[0].wait()
    loads[1].wait()
    t_row = tenant_ref[...]
    t_col = jnp.broadcast_to(t_row.astype(f32), (RD, RD)).T.astype(jnp.int32)
    adv_col = jnp.broadcast_to(adv_ref[...].astype(f32), (RD, RD)).T[:, 0:1]
    o_row = jnp.right_shift(t_row, 3)
    o_col = jnp.right_shift(t_col, 3)
    tl = jnp.bitwise_and(t_col, TEN_DEV - 1).astype(f32).astype(bf16)
    same = o_col == o_row
    earlier_rows = jnp.where(same & (iota((RD, RD), 0) < iota((RD, RD), 1)), 1.0, 0.0)
    rank_row = jnp.sum(earlier_rows, axis=0, keepdims=True).astype(jnp.int32)
    earlier_cols = jnp.where(same & (iota((RD, RD), 1) < iota((RD, RD), 0)), 1.0, 0.0)
    rank_col = jnp.sum(earlier_cols, axis=1, keepdims=True).astype(jnp.int32)
    key8_row = jnp.where(rank_row < SB, o_row * SB + rank_row, -1)
    key9_row = jnp.where(rank_row == SB, o_row, -1)
    o_col1 = o_col[:, 0:1]
    key8_col = jnp.where(rank_col < SB, o_col1 * SB + rank_col, -1)
    key9_col = jnp.where(rank_col == SB, o_col1, -1)
    p8 = one_hot(iota((MR, RD), 0) == key8_row)
    ext_rows = jnp.right_shift(iota((MR, RD), 0), 3) == key9_row
    ext_piece = jnp.bitwise_and(iota((MR, RD), 0), PC - 1)

    def pack9(p):
        return one_hot(ext_rows & (ext_piece == p))

    loads[2].wait()
    b_all[pl.ds(pl.multiple_of(z * BB, BB), BB), :] = (
        bp[...] * ADAPTER_RANK ** (-0.5)
    ).astype(bf16)
    loads[3].wait()
    a_all[pl.ds(pl.multiple_of(z * DB, DB), DB), :] = (
        ap[...] * MODEL_WIDTH ** (-0.5)
    ).astype(bf16)

    loads[4].wait()
    scaled_rows = (cot[...].astype(f32) * (adv_col * 0.25)).astype(bf16)
    scaled[...] = scaled_rows
    ssm[:, 0:KF] = dot_nn(p8, scaled_rows).astype(bf16)
    ssm[:, KF : KF + 128] = dot_nn(p8, tl).astype(bf16)
    misc = jnp.zeros((MR, 128), f32)
    for p in range(PC):
        part9 = scaled_rows[:, 128 * p : 128 * p + 128] if p < 4 else tl
        misc = misc + dot_nn(pack9(p), part9)
    ssm[:, KF + 128 : KF + 256] = misc.astype(bf16)

    pl.semaphore_wait(barrier, ND - 1 + 2)

    def a2a_start(src, dst, c0, cw, i):
        def go(k, carry):
            peer = lax.rem(me + k, ND)
            pltpu.make_async_remote_copy(
                src_ref=src.at[pl.ds(pl.multiple_of(peer * SB, SB), SB), pl.ds(c0, cw)],
                dst_ref=dst.at[pl.ds(pl.multiple_of(me * SB, SB), SB), pl.ds(c0, cw)],
                send_sem=a2a_ss.at[i],
                recv_sem=a2a_rs.at[i],
                device_id=(peer, z),
                device_id_type=MESH,
            ).start()
            return carry

        lax.fori_loop(1, ND, go, 0)
        own = pl.ds(pl.multiple_of(me * SB, SB), SB)
        dst[own, c0 : c0 + cw] = src[own, c0 : c0 + cw]

    def a2a_all(src, dst, c0, cw, i):
        return pltpu.make_async_remote_copy(
            src_ref=src.at[pl.ds(0, MR - SB), pl.ds(c0, cw)],
            dst_ref=dst.at[pl.ds(0, MR - SB), pl.ds(c0, cw)],
            send_sem=a2a_ss.at[i],
            recv_sem=a2a_rs.at[i],
            device_id=(mate, z),
            device_id_type=MESH,
        )

    def gather_copy(buf, ss, rs, rows, off, size, dr, step):
        block = lax.rem(z - step + NZ, NZ) if dr == 0 else lax.rem(z + step, NZ)
        view = buf.at[pl.ds(pl.multiple_of(block * rows + off, size), size), :]
        return pltpu.make_async_remote_copy(
            src_ref=view,
            dst_ref=view,
            send_sem=ss,
            recv_sem=rs,
            device_id=(me, zside[dr]),
            device_id_type=MESH,
        )

    steps = (NZ // 2, NZ // 2 - 1)
    HB = DB // 2

    def a_copy(dr, s, q):
        return gather_copy(
            a_all, ag_ss.at[dr, s, q], ag_rs.at[dr, s, q], DB, q * HB, HB, dr, s
        )

    def b_copy(dr, s):
        return gather_copy(b_all, bg_ss.at[dr, s], bg_rs.at[dr, s], BB, 0, BB, dr, s)

    def w_copy(dr, s):
        src, dst = ((NZ - s) % NZ, NZ - 1 - s) if dr == 0 else (s, s + 1)
        return pltpu.make_async_remote_copy(
            src_ref=w_all.at[quarter, core, src],
            dst_ref=w_all.at[quarter, core, dst],
            send_sem=wg_ss.at[dr, s],
            recv_sem=wg_rs.at[dr, s],
            device_id=(me, zside[dr]),
            device_id_type=MESH,
        )

    def w_span(i, t):
        first, count = W_RANGES[i]
        half = (count + 1) // 2
        return ((first, count), (first, count), (first, half), (first + half, count - half))[t]

    def w_near(i, t):
        first, count = w_span(i, t) if t < 4 else W_RANGES[i]
        view = w_all.at[quarter, core, pl.ds(first, count)]
        return pltpu.make_async_remote_copy(
            src_ref=view,
            dst_ref=view,
            send_sem=wx_ss.at[t, i],
            recv_sem=wx_rs.at[t, i],
            device_id=(near[t] if t < 4 else mate, z),
            device_id_type=MESH,
        )

    def w_mate(i, t):
        first, count = w_span(i, t)
        view = w_all.at[
            lax.rem(quarter + (3, 1, 2, 2)[t], 4), core, pl.ds(first, count)
        ]
        return pltpu.make_async_remote_copy(
            src_ref=view,
            dst_ref=view,
            send_sem=wf_ss.at[t, i],
            recv_sem=wf_rs.at[t, i],
            device_id=(mate, z),
            device_id_type=MESH,
        )

    def w_spread(i):
        for t in range(5):
            w_near(i, t).start()

    def w_forward(i):
        for t in range(4):
            w_near(i, t).wait_recv()
            w_mate(i, t).start()

    def base_block(slot):
        block = lax.rem(z + slot, NZ)
        cols = pl.ds(pl.multiple_of(block * DB, DB), DB)
        rows = jnp.concatenate(
            [w_all[c, k, slot] for c in range(4) for k in range(2)], axis=0
        )
        gi_ref[:, cols] = dot_nt(scaled[...], rows).astype(bf16)

    def base_range(i):
        w_near(i, 4).wait_recv()
        for t in range(4):
            w_mate(i, t).wait_recv()
        first, count = W_RANGES[i]
        for slot in range(first, first + count):
            base_block(slot)

    def ab_step(s):
        for dr in (0, 1):
            if s > 0 and s - 1 < steps[dr]:
                b_copy(dr, s - 1).wait_recv()
            if s < steps[dr]:
                b_copy(dr, s).start()
        for q in (0, 1):
            for dr in (0, 1):
                if s > 0 and s - 1 < steps[dr]:
                    a_copy(dr, s - 1, q).wait_recv()
                if s < steps[dr]:
                    a_copy(dr, s, q).start()
        for dr in (0, 1):
            if s > 0 and s - 1 < steps[dr]:
                w_copy(dr, s - 1).wait_recv()
            if s < steps[dr]:
                w_copy(dr, s).start()

    for i in range(10, 18):
        loads[i].wait()
    ab_step(0)
    a2a_start(ssm, rsm, 0, SMW, 0)
    loads[5].wait()

    def pack_pieces(p, acc):
        cols = pl.ds(pl.multiple_of(p * PW, PW), PW)
        return acc + dot_nn(one_hot(ext_rows & (ext_piece == p)), xb[:, cols])

    def send_acts(ch):
        for h in range(CW // 512):
            c0 = ch * CW + h * 512
            sx[:, c0 : c0 + 512] = dot_nn(p8, xb[:, c0 : c0 + 512]).astype(bf16)
        a2a_start(sx, rx, ch * CW, CW, 1 + ch)

    send_acts(0)
    send_acts(1)
    ab_step(1)
    send_acts(2)
    send_acts(3)
    sxe[...] = lax.fori_loop(0, PC, pack_pieces, jnp.zeros((MR, PW), f32)).astype(bf16)
    a2a_start(sxe, rxe, 0, PW, 1 + NCH)
    ab_step(2)

    def pick9(p):
        return one_hot(iota((ND, MR), 1) == iota((ND, MR), 0) * PC + p)

    a2a_all(ssm, rsm, 0, SMW, 0).wait_recv()
    rs_all[0:MR, :] = rsm[:, 0:KF]
    misc_in = rsm[:, KF + 128 : KF + 256]
    for p in range(4):
        rs_all[MR:AR, 128 * p : 128 * p + 128] = dot_nn(pick9(p), misc_in).astype(bf16)
    t_all = jnp.concatenate(
        [rsm[:, KF : KF + 128].astype(f32), dot_nn(pick9(4), misc_in)], axis=0
    ).astype(jnp.int32)
    mask = jnp.right_shift(iota((AR, CB), 1), 5) == jnp.concatenate([t_all, t_all], axis=1)
    ab_step(3)
    base_block(0)
    ab_step(4)
    w_spread(0)
    w_spread(1)
    for s in range(5, 9):
        ab_step(s)
    back_f = jnp.where(mask, dot_nt(rs_all[...], b_all[...]), 0.0)
    back_s[...] = back_f.astype(bf16)
    back_t[...] = back_f.T.astype(bf16)

    down_coefficient = adapter_scale * MODEL_WIDTH ** (-0.5)
    up_coefficient = adapter_scale * ADAPTER_RANK ** (-0.5)

    rsteps = (NZ // 2, NZ // 2 - 1)

    def target(dr, k):
        return lax.rem(z + NZ - 8 + k, NZ) if dr == 0 else lax.rem(z + 7 - k, NZ)

    def a_partial(block):
        cols = pl.ds(pl.multiple_of(block * DB, DB), DB)
        return down_coefficient * dot_nn(back_t[...], rx[:, cols])

    def rs_copy(dr, k, q):
        rows = pl.ds(q * HB, HB)
        return pltpu.make_async_remote_copy(
            src_ref=ls_send.at[dr, k, rows, :],
            dst_ref=ls_recv.at[dr, k, rows, :],
            send_sem=rs_ss.at[dr, k, q],
            recv_sem=rs_rs.at[dr, k, q],
            device_id=(me, (left, right)[dr]),
            device_id_type=MESH,
        )

    def gb_copy(dr, k):
        return pltpu.make_async_remote_copy(
            src_ref=gs_send.at[dr, k],
            dst_ref=gs_recv.at[dr, k],
            send_sem=gr_ss.at[dr, k],
            recv_sem=gr_rs.at[dr, k],
            device_id=(me, (left, right)[dr]),
            device_id_type=MESH,
        )

    def rs_parts(k):
        for dr in (0, 1):
            if k < rsteps[dr]:
                part[dr] = a_partial(target(dr, k))

    def rs_step(k):
        for q in (0, 1):
            rows = slice(q * HB, q * HB + HB)
            for dr in (0, 1):
                if k < rsteps[dr]:
                    total = part[dr, rows, :]
                    if k > 0:
                        rs_copy(dr, k - 1, q).wait_recv()
                        total = total + ls_recv[dr, k - 1, rows, :].astype(f32)
                    ls_send[dr, k, rows, :] = total.astype(bf16)
                    rs_copy(dr, k, q).start()

    def gb_rows(block):
        return gbp[pl.ds(pl.multiple_of(block * BB, BB), BB), :]

    def gb_step(k):
        for dr in (0, 1):
            if k < rsteps[dr]:
                total = gb_rows(target(dr, k))
                if k > 0:
                    gb_copy(dr, k - 1).wait_recv()
                    total = total + gs_recv[dr, k - 1].astype(f32)
                gs_send[dr, k] = total.astype(bf16)
                gb_copy(dr, k).start()

    def put9(p):
        return one_hot(iota((MR, ND), 0) == iota((MR, ND), 1) * PC + p)

    def side_chunk(ch, acc):
        for h in range(CW // PW):
            p = ch * (CW // PW) + h
            term = (
                adapter_scale * dot_nt(back_s[...], a_all[p * PW : p * PW + PW, :])
            ).astype(bf16)
            sd[:, p * PW : p * PW + PW] = term[0:MR]
            acc = acc + dot_nn(put9(p), term[MR:AR])
        a2a_start(sd, rd, ch * CW, CW, NCH + 2 + ch)
        return acc

    ext = side_chunk(0, jnp.zeros((MR, PW), f32))
    for ch in range(NCH):
        a2a_all(sx, rx, ch * CW, CW, 1 + ch).wait_recv()
    a2a_all(sxe, rxe, 0, PW, 1 + NCH).wait_recv()
    for p in range(PC):
        rx[MR:AR, p * PW : p * PW + PW] = dot_nn(pick9(p), rxe[...]).astype(bf16)
    rs_parts(0)
    rs_step(0)
    w_forward(0)
    w_forward(1)
    mid = dot_nn(rx[...], a_all[...])
    mid_s[...] = jnp.where(mask, mid, 0.0).T.astype(bf16)
    gbp[...] = up_coefficient * dot_nn(mid_s[...], rs_all[...])
    gb_step(0)
    rs_parts(1)
    rs_step(1)
    rs_parts(2)
    ext = side_chunk(1, ext)
    w_spread(2)
    gb_step(1)
    rs_step(2)
    rs_parts(3)
    ext = side_chunk(2, ext)
    w_spread(3)
    gb_step(2)
    rs_step(3)
    rs_parts(4)
    ext = side_chunk(3, ext)
    se[...] = ext.astype(bf16)
    a2a_start(se, rde, 0, PW, 2 * NCH + 2)
    gb_step(3)
    rs_step(4)
    rs_parts(5)
    gb_step(4)
    base_range(0)
    rs_step(5)
    rs_parts(6)
    gb_step(5)
    base_range(1)
    rs_step(6)
    rs_parts(7)
    gb_step(6)
    w_forward(2)
    w_forward(3)
    rs_step(7)
    gb_step(7)
    base_range(2)
    base_range(3)
    r8 = one_hot(iota((RD, MR), 1) == key8_col)
    back_rows = jnp.right_shift(iota((RD, MR), 1), 3) == key9_col
    back_piece = jnp.bitwise_and(iota((RD, MR), 1), PC - 1)
    for ch in range(NCH):
        a2a_all(sd, rd, ch * CW, CW, NCH + 2 + ch).wait_recv()
    a2a_all(se, rde, 0, PW, 2 * NCH + 2).wait_recv()
    for p in range(PC):
        cols = slice(p * PW, p * PW + PW)
        r9 = one_hot(back_rows & (back_piece == p))
        side_rows = (dot_nn(r8, rd[:, cols]) + dot_nn(r9, rde[...])).astype(bf16)
        gi_ref[:, cols] = (gi_ref[:, cols].astype(f32) + side_rows.astype(f32)).astype(bf16)

    total = a_partial(z)
    for q in (0, 1):
        for dr in (0, 1):
            rs_copy(dr, rsteps[dr] - 1, q).wait_recv()
    total = total + ls_recv[0, rsteps[0] - 1].astype(f32)
    total = total + ls_recv[1, rsteps[1] - 1].astype(f32)
    for i in range(6, 10):
        loads[i].wait()
    adam_refs(ap, am, av, total.T, ap_out, am_out, av_out)
    for dr in (0, 1):
        gb_copy(dr, rsteps[dr] - 1).wait_recv()
    total_b = (
        gb_rows(z)
        + gs_recv[0, rsteps[0] - 1].astype(f32)
        + gs_recv[1, rsteps[1] - 1].astype(f32)
    )
    adam_refs(bp, bm, bv, total_b, bp_out, bm_out, bv_out)

    a2a_all(ssm, rsm, 0, SMW, 0).wait_send()
    for ch in range(NCH):
        a2a_all(sx, rx, ch * CW, CW, 1 + ch).wait_send()
        a2a_all(sd, rd, ch * CW, CW, NCH + 2 + ch).wait_send()
    a2a_all(sxe, rxe, 0, PW, 1 + NCH).wait_send()
    a2a_all(se, rde, 0, PW, 2 * NCH + 2).wait_send()
    for i in range(len(W_RANGES)):
        for t in range(5):
            w_near(i, t).wait_send()
        for t in range(4):
            w_mate(i, t).wait_send()
    for dr in (0, 1):
        for s in range(steps[dr]):
            for q in (0, 1):
                a_copy(dr, s, q).wait_send()
            b_copy(dr, s).wait_send()
            w_copy(dr, s).wait_send()
        for k in range(rsteps[dr]):
            for q in (0, 1):
                rs_copy(dr, k, q).wait_send()
            gb_copy(dr, k).wait_send()


def finish_kernel(*refs):
    n = len(refs) // 2
    sems = refs[-1]
    copies = [pltpu.make_async_copy(refs[i], refs[n + i], sems.at[i]) for i in range(n)]
    for copy in copies:
        copy.start()
    for copy in copies:
        copy.wait()


def per_device(
    acts,
    cotangent,
    tenant,
    advantage,
    base_weight,
    a_param,
    a_moment,
    a_second,
    b_param,
    b_moment,
    b_second,
):
    vmem = pl.BlockSpec(memory_space=pltpu.VMEM)
    hbm = pl.BlockSpec(memory_space=pltpu.HBM)
    dma = pltpu.SemaphoreType.DMA
    v = pltpu.VMEM
    out_shape = (
        jax.ShapeDtypeStruct((RD, D), bf16),
        *[jax.ShapeDtypeStruct((DB, CB), f32)] * 3,
        *[jax.ShapeDtypeStruct((BB, KF), f32)] * 3,
    )
    results = pl.pallas_call(
        exchange_kernel,
        out_shape=out_shape,
        in_specs=[hbm] * 11,
        out_specs=(vmem,) * 7,
        scratch_shapes=[
            v((1, RD), jnp.int32),
            v((1, RD), jnp.int32),
            v((RD, D), bf16),
            v((RD, KF), bf16),
            v((DB, CB), f32),
            v((DB, CB), f32),
            v((DB, CB), f32),
            v((BB, KF), f32),
            v((BB, KF), f32),
            v((BB, KF), f32),
            v((MR, D), bf16),
            v((MR, PW), bf16),
            v((MR, SMW), bf16),
            v((AR, D), bf16),
            v((MR, PW), bf16),
            v((MR, SMW), bf16),
            v((AR, KF), bf16),
            v((RD, KF), bf16),
            v((D, CB), bf16),
            v((CB, KF), bf16),
            v((4, 2, NZ, WR, KF), bf16),
            v((AR, CB), bf16),
            v((CB, AR), bf16),
            v((CB, AR), bf16),
            v((CB, KF), f32),
            v((2, CB, DB), f32),
            v((MR, D), bf16),
            v((MR, PW), bf16),
            v((MR, D), bf16),
            v((MR, PW), bf16),
            v((2, 8, CB, DB), bf16),
            v((2, 8, CB, DB), bf16),
            v((2, 8, BB, KF), bf16),
            v((2, 8, BB, KF), bf16),
            dma((18,)),
            dma((2 * NCH + 3,)),
            dma((2 * NCH + 3,)),
            dma((2, 8, 2)),
            dma((2, 8, 2)),
            dma((2, 8)),
            dma((2, 8)),
            dma((2, 8)),
            dma((2, 8)),
            dma((5, 4)),
            dma((5, 4)),
            dma((4, 4)),
            dma((4, 4)),
            dma((2, 8, 2)),
            dma((2, 8, 2)),
            dma((2, 8)),
            dma((2, 8)),
        ],
        compiler_params=pltpu.CompilerParams(
            collective_id=0, has_side_effects=True, vmem_limit_bytes=48 * 1024 * 1024
        ),
        name="exchange",
    )(
        *[
            pltpu.with_memory_space_constraint(x, pltpu.HBM)
            for x in (
                tenant.reshape(1, RD),
                advantage.reshape(1, RD),
                acts,
                cotangent,
                base_weight,
                a_param,
                a_moment,
                a_second,
                b_param,
                b_moment,
                b_second,
            )
        ]
    )
    return tuple(
        pl.pallas_call(
            finish_kernel,
            out_shape=out_shape,
            in_specs=[vmem] * 7,
            out_specs=(hbm,) * 7,
            scratch_shapes=[dma((7,))],
            compiler_params=pltpu.CompilerParams(vmem_limit_bytes=1024 * 1024),
            name="finish",
        )(*results)
    )


def solution(mesh):
    in_specs = (
        P(("dp", "fsdp"), None),
        P(("dp", "fsdp"), None),
        P(("dp", "fsdp")),
        P(("dp", "fsdp")),
        P("fsdp", None),
        P("fsdp", "dp"),
        P("fsdp", "dp"),
        P("fsdp", "dp"),
        P(("dp", "fsdp"), None),
        P(("dp", "fsdp"), None),
        P(("dp", "fsdp"), None),
    )
    out_specs = (
        P(("dp", "fsdp"), None),
        P("fsdp", "dp"),
        P("fsdp", "dp"),
        P("fsdp", "dp"),
        P(("dp", "fsdp"), None),
        P(("dp", "fsdp"), None),
        P(("dp", "fsdp"), None),
    )
    return jax.shard_map(
        per_device, mesh=mesh, in_specs=in_specs, out_specs=out_specs, check_vma=False
    )
```

```python
import functools

import jax
import jax.numpy as jnp
from jax import lax
from jax.experimental import pallas as pl
from jax.experimental.pallas import tpu as pltpu
from jax.sharding import PartitionSpec as P

MODEL_WIDTH = 4096
ADAPTER_RANK = 32
TEN_DEV = 8
MESH = pl.DeviceIdType.MESH

adapter_scale = 2.0
learn_rate = 0.02
beta_one = 0.9
beta_two = 0.999
adam_eps = 1e-08
bias_one = 1.0 - 0.9**10
bias_two = 1.0 - 0.999**10

ND = 32
NZ = 16
D = MODEL_WIDTH
KF = 512
RD = 128
CB = TEN_DEV * ADAPTER_RANK
SB = 8
MR = ND * SB
AR = MR + ND
PC = 8
PW = D // PC
DB = D // NZ
BB = CB // NZ
SMW = KF + 256
WR = DB // 8
W_RANGES = ((1, 4), (12, 4), (5, 3), (8, 4))

bf16 = jnp.bfloat16
f32 = jnp.float32


def dot_nn(a, b):
    return lax.dot_general(a, b, (((1,), (0,)), ((), ())), preferred_element_type=f32)


def dot_nt(a, b):
    return lax.dot_general(a, b, (((1,), (1,)), ((), ())), preferred_element_type=f32)


def one_hot(cond):
    return jnp.where(cond, 1.0, 0.0).astype(bf16)


def iota(shape, dim):
    return lax.broadcasted_iota(jnp.int32, shape, dim)


def adam_refs(param, moment, second, gradient, out_param, out_moment, out_second):
    new_moment = beta_one * moment[...] + (1.0 - beta_one) * gradient
    new_second = beta_two * second[...] + (1.0 - beta_two) * gradient * gradient
    out_moment[...] = new_moment
    out_second[...] = new_second
    out_param[...] = param[...] - learn_rate * (new_moment / bias_one) / (
        jnp.sqrt(new_second / bias_two) + adam_eps
    )


def exchange_kernel(
    tenant_hbm,
    adv_hbm,
    acts_hbm,
    cot_hbm,
    w_hbm,
    ap_hbm,
    am_hbm,
    av_hbm,
    bp_hbm,
    bm_hbm,
    bv_hbm,
    gi_ref,
    ap_out,
    am_out,
    av_out,
    bp_out,
    bm_out,
    bv_out,
    tenant_ref,
    adv_ref,
    xb,
    cot,
    ap,
    am,
    av,
    bp,
    bm,
    bv,
    sx,
    sxe,
    ssm,
    rx,
    rxe,
    rsm,
    rs_all,
    scaled,
    a_all,
    b_all,
    w_all,
    back_s,
    back_t,
    mid_s,
    gbp,
    part,
    sd,
    se,
    rd,
    rde,
    ls_send,
    ls_recv,
    gs_send,
    gs_recv,
    loc_sem,
    a2a_ss,
    a2a_rs,
    ag_ss,
    ag_rs,
    bg_ss,
    bg_rs,
    wg_ss,
    wg_rs,
    wx_ss,
    wx_rs,
    wf_ss,
    wf_rs,
    rs_ss,
    rs_rs,
    gr_ss,
    gr_rs,
):
    me = lax.axis_index("dp")
    z = lax.axis_index("fsdp")
    core = lax.rem(me, 2)
    mate = me + 1 - 2 * core
    x = me // 8
    y = lax.rem(me // 2, 4)
    quarter = lax.rem(x * (1 + core) + y * (2 - core), 4)

    def chip(cx, cy):
        return (lax.rem(cx, 4) * 4 + lax.rem(cy, 4)) * 2 + core

    near = (
        chip(x + 1 - core, y + core),
        chip(x + 3 * (1 - core), y + 3 * core),
        chip(x + core, y + 1 - core),
        chip(x + 3 * core, y + 3 * (1 - core)),
    )
    right = lax.rem(z + 1, NZ)
    left = lax.rem(z + NZ - 1, NZ)
    zside = (right, left)
    zfar = (lax.rem(z + 4, NZ), lax.rem(z + NZ - 4, NZ))

    loads = [
        pltpu.make_async_copy(src, dst, loc_sem.at[i])
        for i, (src, dst) in enumerate(
            [
                (tenant_hbm, tenant_ref),
                (adv_hbm, adv_ref),
                (bp_hbm, bp),
                (ap_hbm, ap),
                (cot_hbm, cot),
                (am_hbm, am),
                (av_hbm, av),
                (bm_hbm, bm),
                (bv_hbm, bv),
                *[
                    (
                        w_hbm.at[(2 * c + k) * WR : (2 * c + k + 1) * WR, :],
                        w_all.at[c, k, 0],
                    )
                    for c in range(4)
                    for k in range(2)
                ],
                *[
                    (
                        acts_hbm.at[:, pl.ds(pl.multiple_of(lax.rem(z + r, NZ) * DB, DB), DB)],
                        xb.at[:, r * DB : r * DB + DB],
                    )
                    for r in range(NZ)
                ],
            ]
        )
    ]
    for load in loads:
        load.start()
    barrier = pltpu.get_barrier_semaphore()

    def greet(k, carry):
        pl.semaphore_signal(
            barrier, inc=1, device_id=(lax.rem(me + k, ND), z), device_id_type=MESH
        )
        return carry

    lax.fori_loop(1, ND, greet, 0)
    for side in (*zside, *zfar):
        pl.semaphore_signal(barrier, inc=1, device_id=(me, side), device_id_type=MESH)

    loads[2].wait()
    b_all[pl.ds(pl.multiple_of(z * BB, BB), BB), :] = (
        bp[...] * ADAPTER_RANK ** (-0.5)
    ).astype(bf16)
    loads[3].wait()
    a_all[0:DB, :] = (
        ap[...] * MODEL_WIDTH ** (-0.5)
    ).astype(bf16)

    loads[0].wait()
    loads[1].wait()
    t_row = tenant_ref[...]
    t_col = jnp.broadcast_to(t_row.astype(f32), (RD, RD)).T.astype(jnp.int32)
    adv_col = jnp.broadcast_to(adv_ref[...].astype(f32), (RD, RD)).T[:, 0:1]
    o_row = jnp.right_shift(t_row, 3)
    o_col = jnp.right_shift(t_col, 3)
    tl = jnp.bitwise_and(t_col, TEN_DEV - 1).astype(f32).astype(bf16)
    same = o_col == o_row
    earlier_rows = jnp.where(same & (iota((RD, RD), 0) < iota((RD, RD), 1)), 1.0, 0.0)
    rank_row = jnp.sum(earlier_rows, axis=0, keepdims=True).astype(jnp.int32)
    earlier_cols = jnp.where(same & (iota((RD, RD), 1) < iota((RD, RD), 0)), 1.0, 0.0)
    rank_col = jnp.sum(earlier_cols, axis=1, keepdims=True).astype(jnp.int32)
    key8_row = jnp.where(rank_row < SB, o_row * SB + rank_row, -1)
    key9_row = jnp.where(rank_row == SB, o_row, -1)
    o_col1 = o_col[:, 0:1]
    key8_col = jnp.where(rank_col < SB, o_col1 * SB + rank_col, -1)
    key9_col = jnp.where(rank_col == SB, o_col1, -1)
    p8 = one_hot(iota((MR, RD), 0) == key8_row)
    ext_rows = jnp.right_shift(iota((MR, RD), 0), 3) == key9_row
    ext_piece = jnp.bitwise_and(iota((MR, RD), 0), PC - 1)

    def pack9(p):
        return one_hot(ext_rows & (ext_piece == p))

    pl.semaphore_wait(barrier, ND - 1 + 4)

    def a2a_start(src, dst, c0, cw, i):
        def go(k, carry):
            peer = lax.rem(me + k, ND)
            pltpu.make_async_remote_copy(
                src_ref=src.at[pl.ds(pl.multiple_of(peer * SB, SB), SB), pl.ds(c0, cw)],
                dst_ref=dst.at[pl.ds(pl.multiple_of(me * SB, SB), SB), pl.ds(c0, cw)],
                send_sem=a2a_ss.at[i],
                recv_sem=a2a_rs.at[i],
                device_id=(peer, z),
                device_id_type=MESH,
            ).start()
            return carry

        lax.fori_loop(1, ND, go, 0)
        own = pl.ds(pl.multiple_of(me * SB, SB), SB)
        dst[own, c0 : c0 + cw] = src[own, c0 : c0 + cw]

    def a2a_all(src, dst, c0, cw, i):
        return pltpu.make_async_remote_copy(
            src_ref=src.at[pl.ds(0, MR - SB), pl.ds(c0, cw)],
            dst_ref=dst.at[pl.ds(0, MR - SB), pl.ds(c0, cw)],
            send_sem=a2a_ss.at[i],
            recv_sem=a2a_rs.at[i],
            device_id=(mate, z),
            device_id_type=MESH,
        )

    steps = (NZ // 2, NZ // 2 - 1)
    HB = DB // 2

    def a_copy(dr, s, q):
        src, dst = ((NZ - s) % NZ, NZ - 1 - s) if dr == 0 else (s, s + 1)
        return pltpu.make_async_remote_copy(
            src_ref=a_all.at[pl.ds(src * DB + q * HB, HB), :],
            dst_ref=a_all.at[pl.ds(dst * DB + q * HB, HB), :],
            send_sem=ag_ss.at[dr, s, q],
            recv_sem=ag_rs.at[dr, s, q],
            device_id=(me, zside[dr]),
            device_id_type=MESH,
        )

    def b_copy(dr, dist):
        block = lax.rem(z + (NZ - dist % 8 if dr == 0 else dist % 8), NZ)
        view = b_all.at[pl.ds(pl.multiple_of(block * BB, BB), BB), :]
        return pltpu.make_async_remote_copy(
            src_ref=view,
            dst_ref=view,
            send_sem=bg_ss.at[dr, dist],
            recv_sem=bg_rs.at[dr, dist],
            device_id=(me, zfar[dr] if dist == 8 else zside[dr]),
            device_id_type=MESH,
        )

    b_plan = (
        ((), (0, 8)),
        ((0, 8), (1, 4)),
        ((1, 4), (2, 5)),
        ((2, 5), (6,)),
        ((6,), (7,)),
        ((7,), ()),
    )
    b_sent = ((0, 8, 1, 4, 2, 5, 6, 7), (0, 8, 1, 4, 2, 5, 6))

    def w_copy(dr, s):
        src, dst = ((NZ - s) % NZ, NZ - 1 - s) if dr == 0 else (s, s + 1)
        return pltpu.make_async_remote_copy(
            src_ref=w_all.at[quarter, core, src],
            dst_ref=w_all.at[quarter, core, dst],
            send_sem=wg_ss.at[dr, s],
            recv_sem=wg_rs.at[dr, s],
            device_id=(me, zside[dr]),
            device_id_type=MESH,
        )

    def w_span(i, t):
        first, count = W_RANGES[i]
        half = (count + 1) // 2
        return ((first, count), (first, count), (first, half), (first + half, count - half))[t]

    def w_near(i, t):
        first, count = w_span(i, t) if t < 4 else W_RANGES[i]
        view = w_all.at[quarter, core, pl.ds(first, count)]
        return pltpu.make_async_remote_copy(
            src_ref=view,
            dst_ref=view,
            send_sem=wx_ss.at[t, i],
            recv_sem=wx_rs.at[t, i],
            device_id=(near[t] if t < 4 else mate, z),
            device_id_type=MESH,
        )

    def w_mate(i, t):
        first, count = w_span(i, t)
        view = w_all.at[
            lax.rem(quarter + (3, 1, 2, 2)[t], 4), core, pl.ds(first, count)
        ]
        return pltpu.make_async_remote_copy(
            src_ref=view,
            dst_ref=view,
            send_sem=wf_ss.at[t, i],
            recv_sem=wf_rs.at[t, i],
            device_id=(mate, z),
            device_id_type=MESH,
        )

    def w_spread(i):
        for t in range(5):
            w_near(i, t).start()

    def w_forward(i):
        for t in range(4):
            w_near(i, t).wait_recv()
            w_mate(i, t).start()

    def base_block(slot):
        block = lax.rem(z + slot, NZ)
        cols = pl.ds(pl.multiple_of(block * DB, DB), DB)
        rows = jnp.concatenate(
            [w_all[c, k, slot] for c in range(4) for k in range(2)], axis=0
        )
        gi_ref[:, cols] = dot_nt(scaled[...], rows).astype(bf16)

    def base_range(i):
        w_near(i, 4).wait_recv()
        for t in range(4):
            w_mate(i, t).wait_recv()
        first, count = W_RANGES[i]
        for slot in range(first, first + count):
            base_block(slot)

    def ab_step(s):
        if s < len(b_plan):
            for dr in (0, 1):
                for dist in b_plan[s][0]:
                    if dist in b_sent[dr]:
                        b_copy(dr, dist).wait_recv()
                for dist in b_plan[s][1]:
                    if dist in b_sent[dr]:
                        b_copy(dr, dist).start()
        for q in (0, 1):
            for dr in (0, 1):
                if s > 0 and s - 1 < steps[dr]:
                    a_copy(dr, s - 1, q).wait_recv()
                if s < steps[dr]:
                    a_copy(dr, s, q).start()
        for dr in (0, 1):
            if s > 0 and s - 1 < steps[dr]:
                w_copy(dr, s - 1).wait_recv()
            if s < steps[dr]:
                w_copy(dr, s).start()

    down_coefficient = adapter_scale * MODEL_WIDTH ** (-0.5)
    up_coefficient = adapter_scale * ADAPTER_RANK ** (-0.5)

    rsteps = (NZ // 2, NZ // 2 - 1)

    def a_partial(slot):
        return down_coefficient * dot_nn(back_t[...], rx[:, slot * DB : slot * DB + DB])

    def rs_copy(dr, k, q):
        rows = pl.ds(q * HB, HB)
        return pltpu.make_async_remote_copy(
            src_ref=ls_send.at[dr, k, rows, :],
            dst_ref=ls_recv.at[dr, k, rows, :],
            send_sem=rs_ss.at[dr, k, q],
            recv_sem=rs_rs.at[dr, k, q],
            device_id=(me, (left, right)[dr]),
            device_id_type=MESH,
        )

    def rs_parts(k):
        for dr in (0, 1):
            if k < rsteps[dr]:
                part[dr] = a_partial(8 + k if dr == 0 else 7 - k)

    def rs_step(k):
        for q in (0, 1):
            rows = slice(q * HB, q * HB + HB)
            for dr in (0, 1):
                if k < rsteps[dr]:
                    total = part[dr, rows, :]
                    if k > 0:
                        rs_copy(dr, k - 1, q).wait_recv()
                        total = total + ls_recv[dr, k - 1, rows, :].astype(f32)
                    ls_send[dr, k, rows, :] = total.astype(bf16)
                    rs_copy(dr, k, q).start()

    def gb_rows(slot):
        block = lax.rem(z + slot, NZ)
        return gbp[pl.ds(pl.multiple_of(block * BB, BB), BB), :]

    def gb_copy(dr, dist):
        return pltpu.make_async_remote_copy(
            src_ref=gs_send.at[dr, dist - 1],
            dst_ref=gs_recv.at[dr, dist - 1],
            send_sem=gr_ss.at[dr, dist - 1],
            recv_sem=gr_rs.at[dr, dist - 1],
            device_id=(me, (zfar[1 - dr] if dist == 4 else (left, right)[dr])),
            device_id_type=MESH,
        )

    def gb_send(dr, dist):
        total = gb_rows(NZ - dist if dr == 0 else dist)
        if dist not in (3, 8 if dr == 0 else 7):
            gb_copy(dr, dist + 1).wait_recv()
            total = total + gs_recv[dr, dist].astype(f32)
        gs_send[dr, dist - 1] = total.astype(bf16)
        gb_copy(dr, dist).start()

    gb_plan = (((8, 3), (7, 3)), ((7, 2), (6, 2)), ((6, 1), (5, 1)), ((5,), (4,)), ((4,), ()))

    def gb_step(k):
        for dr in (0, 1):
            for dist in gb_plan[k][dr]:
                gb_send(dr, dist)

    def put9(p):
        return one_hot(iota((MR, ND), 0) == iota((MR, ND), 1) * PC + p)

    def side_pair(p, acc):
        term = (
            adapter_scale * dot_nt(back_s[...], a_all[p * PW : p * PW + PW, :])
        ).astype(bf16)
        sd[:, p * PW : p * PW + PW] = term[0:MR]
        a2a_start(sd, rd, p * PW, PW, 10 + p)
        return acc + dot_nn(put9(p), term[MR:AR])

    def pick9(p):
        return one_hot(iota((ND, MR), 1) == iota((ND, MR), 0) * PC + p)

    def acts_pair(p):
        sx[:, p * PW : p * PW + PW] = dot_nn(p8, xb[:, p * PW : p * PW + PW]).astype(bf16)
        a2a_start(sx, rx, p * PW, PW, 2 + p)

    def acts_wait(*pairs):
        for p in pairs:
            a2a_all(sx, rx, p * PW, PW, 2 + p).wait_recv()

    for i in range(9, 17):
        loads[i].wait()
    ab_step(0)
    loads[4].wait()
    scaled_rows = (cot[...].astype(f32) * (adv_col * 0.25)).astype(bf16)
    scaled[...] = scaled_rows
    ssm[:, 0:KF] = dot_nn(p8, scaled_rows).astype(bf16)
    ssm[:, KF : KF + 128] = dot_nn(p8, tl).astype(bf16)
    misc = jnp.zeros((MR, 128), f32)
    for p in range(PC):
        part9 = scaled_rows[:, 128 * p : 128 * p + 128] if p < 4 else tl
        misc = misc + dot_nn(pack9(p), part9)
    ssm[:, KF + 128 : KF + 256] = misc.astype(bf16)

    a2a_start(ssm, rsm, 0, SMW, 0)
    for i in range(17, 17 + NZ):
        loads[i].wait()

    def pack_pieces(p, acc):
        cols = pl.ds(pl.multiple_of(p * PW, PW), PW)
        return acc + dot_nn(one_hot(ext_rows & (ext_piece == p)), xb[:, cols])

    sxe[...] = lax.fori_loop(0, PC, pack_pieces, jnp.zeros((MR, PW), f32)).astype(bf16)
    a2a_start(sxe, rxe, 0, PW, 1)
    acts_pair(3)
    acts_pair(4)
    ab_step(1)
    acts_pair(5)
    acts_pair(2)
    acts_pair(6)
    acts_pair(1)
    ab_step(2)
    acts_pair(7)
    acts_pair(0)

    a2a_all(ssm, rsm, 0, SMW, 0).wait_recv()
    rs_all[0:MR, :] = rsm[:, 0:KF]
    misc_in = rsm[:, KF + 128 : KF + 256]
    for p in range(4):
        rs_all[MR:AR, 128 * p : 128 * p + 128] = dot_nn(pick9(p), misc_in).astype(bf16)
    t_all = jnp.concatenate(
        [rsm[:, KF : KF + 128].astype(f32), dot_nn(pick9(4), misc_in)], axis=0
    ).astype(jnp.int32)
    mask = jnp.right_shift(iota((AR, CB), 1), 5) == jnp.concatenate([t_all, t_all], axis=1)
    ab_step(3)
    base_block(0)
    ab_step(4)
    w_spread(0)
    w_spread(1)
    ab_step(5)
    back_f = jnp.where(mask, dot_nt(rs_all[...], b_all[...]), 0.0)
    back_s[...] = back_f.astype(bf16)
    back_t[...] = back_f.T.astype(bf16)
    ext = side_pair(0, jnp.zeros((MR, PW), f32))
    a2a_all(sxe, rxe, 0, PW, 1).wait_recv()
    for p in range(PC):
        rx[MR:AR, p * PW : p * PW + PW] = dot_nn(pick9(p), rxe[...]).astype(bf16)
    acts_wait(3, 4)
    rs_parts(0)
    rs_step(0)
    ext = side_pair(7, ext)
    ab_step(6)
    rs_parts(1)
    rs_step(1)
    ext = side_pair(1, ext)
    ext = side_pair(6, ext)
    ab_step(7)
    acts_wait(5, 2)
    rs_parts(2)
    rs_step(2)
    ext = side_pair(2, ext)
    ext = side_pair(5, ext)
    ab_step(8)
    rs_parts(3)
    rs_step(3)
    ext = side_pair(3, ext)
    ext = side_pair(4, ext)
    se[...] = ext.astype(bf16)
    a2a_start(se, rde, 0, PW, 18)
    w_spread(2)
    w_spread(3)
    acts_wait(6, 1)
    rs_parts(4)
    acts_wait(7, 0)
    mid = dot_nn(rx[...], a_all[...])
    mid_s[...] = jnp.where(mask, mid, 0.0).T.astype(bf16)
    gbp[...] = up_coefficient * dot_nn(mid_s[...], rs_all[...])
    gb_step(0)
    rs_step(4)
    rs_parts(5)
    gb_step(1)
    rs_step(5)
    rs_parts(6)
    w_forward(0)
    w_forward(1)
    gb_step(2)
    rs_step(6)
    rs_parts(7)
    gb_step(3)
    rs_step(7)
    gb_step(4)
    base_range(0)
    base_range(1)
    w_forward(2)
    w_forward(3)
    base_range(2)
    base_range(3)
    r8 = one_hot(iota((RD, MR), 1) == key8_col)
    back_rows = jnp.right_shift(iota((RD, MR), 1), 3) == key9_col
    back_piece = jnp.bitwise_and(iota((RD, MR), 1), PC - 1)
    for p in range(PC):
        a2a_all(sd, rd, p * PW, PW, 10 + p).wait_recv()
    a2a_all(se, rde, 0, PW, 18).wait_recv()
    for p in range(PC):
        r9 = one_hot(back_rows & (back_piece == p))
        side_rows = dot_nn(r8, rd[:, p * PW : p * PW + PW]) + dot_nn(r9, rde[...])
        side_rows = side_rows.astype(bf16).astype(f32)
        for h in (0, 1):
            block = lax.rem(z + 2 * p + h, NZ)
            cols = pl.ds(pl.multiple_of(block * DB, DB), DB)
            gi_ref[:, cols] = (
                gi_ref[:, cols].astype(f32) + side_rows[:, h * DB : h * DB + DB]
            ).astype(bf16)

    total = a_partial(0)
    for q in (0, 1):
        for dr in (0, 1):
            rs_copy(dr, rsteps[dr] - 1, q).wait_recv()
    total = total + ls_recv[0, rsteps[0] - 1].astype(f32)
    total = total + ls_recv[1, rsteps[1] - 1].astype(f32)
    for i in range(5, 9):
        loads[i].wait()
    adam_refs(ap, am, av, total.T, ap_out, am_out, av_out)
    total_b = gb_rows(0)
    for dr in (0, 1):
        for dist in (1, 4):
            gb_copy(dr, dist).wait_recv()
            total_b = total_b + gs_recv[dr, dist - 1].astype(f32)
    adam_refs(bp, bm, bv, total_b, bp_out, bm_out, bv_out)

    a2a_all(ssm, rsm, 0, SMW, 0).wait_send()
    for p in range(PC):
        a2a_all(sx, rx, p * PW, PW, 2 + p).wait_send()
        a2a_all(sd, rd, p * PW, PW, 10 + p).wait_send()
    a2a_all(sxe, rxe, 0, PW, 1).wait_send()
    a2a_all(se, rde, 0, PW, 18).wait_send()
    for i in range(len(W_RANGES)):
        for t in range(5):
            w_near(i, t).wait_send()
        for t in range(4):
            w_mate(i, t).wait_send()
    for dr in (0, 1):
        for s in range(steps[dr]):
            for q in (0, 1):
                a_copy(dr, s, q).wait_send()
            w_copy(dr, s).wait_send()
        for k in range(rsteps[dr]):
            for q in (0, 1):
                rs_copy(dr, k, q).wait_send()
            gb_copy(dr, k + 1).wait_send()
        for dist in b_sent[dr]:
            b_copy(dr, dist).wait_send()


def finish_kernel(*refs):
    n = len(refs) // 2
    sems = refs[-1]
    copies = [pltpu.make_async_copy(refs[i], refs[n + i], sems.at[i]) for i in range(n)]
    for copy in copies:
        copy.start()
    for copy in copies:
        copy.wait()


def per_device(
    acts,
    cotangent,
    tenant,
    advantage,
    base_weight,
    a_param,
    a_moment,
    a_second,
    b_param,
    b_moment,
    b_second,
):
    vmem = pl.BlockSpec(memory_space=pltpu.VMEM)
    hbm = pl.BlockSpec(memory_space=pltpu.HBM)
    dma = pltpu.SemaphoreType.DMA
    v = pltpu.VMEM
    out_shape = (
        jax.ShapeDtypeStruct((RD, D), bf16),
        *[jax.ShapeDtypeStruct((DB, CB), f32)] * 3,
        *[jax.ShapeDtypeStruct((BB, KF), f32)] * 3,
    )
    results = pl.pallas_call(
        exchange_kernel,
        out_shape=out_shape,
        in_specs=[hbm] * 11,
        out_specs=(vmem,) * 7,
        scratch_shapes=[
            v((1, RD), jnp.int32),
            v((1, RD), jnp.int32),
            v((RD, D), bf16),
            v((RD, KF), bf16),
            v((DB, CB), f32),
            v((DB, CB), f32),
            v((DB, CB), f32),
            v((BB, KF), f32),
            v((BB, KF), f32),
            v((BB, KF), f32),
            v((MR, D), bf16),
            v((MR, PW), bf16),
            v((MR, SMW), bf16),
            v((AR, D), bf16),
            v((MR, PW), bf16),
            v((MR, SMW), bf16),
            v((AR, KF), bf16),
            v((RD, KF), bf16),
            v((D, CB), bf16),
            v((CB, KF), bf16),
            v((4, 2, NZ, WR, KF), bf16),
            v((AR, CB), bf16),
            v((CB, AR), bf16),
            v((CB, AR), bf16),
            v((CB, KF), f32),
            v((2, CB, DB), f32),
            v((MR, D), bf16),
            v((MR, PW), bf16),
            v((MR, D), bf16),
            v((MR, PW), bf16),
            v((2, 8, CB, DB), bf16),
            v((2, 8, CB, DB), bf16),
            v((2, 8, BB, KF), bf16),
            v((2, 8, BB, KF), bf16),
            dma((17 + NZ,)),
            dma((19,)),
            dma((19,)),
            dma((2, 8, 2)),
            dma((2, 8, 2)),
            dma((2, 9)),
            dma((2, 9)),
            dma((2, 8)),
            dma((2, 8)),
            dma((5, 4)),
            dma((5, 4)),
            dma((4, 4)),
            dma((4, 4)),
            dma((2, 8, 2)),
            dma((2, 8, 2)),
            dma((2, 8)),
            dma((2, 8)),
        ],
        compiler_params=pltpu.CompilerParams(
            collective_id=0, has_side_effects=True, vmem_limit_bytes=48 * 1024 * 1024
        ),
        name="exchange",
    )(
        *[
            pltpu.with_memory_space_constraint(x, pltpu.HBM)
            for x in (
                tenant.reshape(1, RD),
                advantage.reshape(1, RD),
                acts,
                cotangent,
                base_weight,
                a_param,
                a_moment,
                a_second,
                b_param,
                b_moment,
                b_second,
            )
        ]
    )
    return tuple(
        pl.pallas_call(
            finish_kernel,
            out_shape=out_shape,
            in_specs=[vmem] * 7,
            out_specs=(hbm,) * 7,
            scratch_shapes=[dma((7,))],
            compiler_params=pltpu.CompilerParams(vmem_limit_bytes=1024 * 1024),
            name="finish",
        )(*results)
    )


def solution(mesh):
    in_specs = (
        P(("dp", "fsdp"), None),
        P(("dp", "fsdp"), None),
        P(("dp", "fsdp")),
        P(("dp", "fsdp")),
        P("fsdp", None),
        P("fsdp", "dp"),
        P("fsdp", "dp"),
        P("fsdp", "dp"),
        P(("dp", "fsdp"), None),
        P(("dp", "fsdp"), None),
        P(("dp", "fsdp"), None),
    )
    out_specs = (
        P(("dp", "fsdp"), None),
        P("fsdp", "dp"),
        P("fsdp", "dp"),
        P("fsdp", "dp"),
        P(("dp", "fsdp"), None),
        P(("dp", "fsdp"), None),
        P(("dp", "fsdp"), None),
    )
    return jax.shard_map(
        per_device, mesh=mesh, in_specs=in_specs, out_specs=out_specs, check_vma=False
    )
```

```python
import functools

import jax
import jax.numpy as jnp
from jax import lax
from jax.experimental import pallas as pl
from jax.experimental.pallas import tpu as pltpu
from jax.sharding import PartitionSpec as P

MODEL_WIDTH = 4096
ADAPTER_RANK = 32
TEN_DEV = 8
MESH = pl.DeviceIdType.MESH

adapter_scale = 2.0
learn_rate = 0.02
beta_one = 0.9
beta_two = 0.999
adam_eps = 1e-08
bias_one = 1.0 - 0.9**10
bias_two = 1.0 - 0.999**10

ND = 32
NZ = 16
D = MODEL_WIDTH
KF = 512
RD = 128
CB = TEN_DEV * ADAPTER_RANK
SB = 8
MR = ND * SB
AR = MR + ND
PC = 8
PW = D // PC
DB = D // NZ
BB = CB // NZ
SMW = KF + 256
WR = DB // 8
W_RANGES = ((1, 4), (12, 4), (5, 3), (8, 4))

bf16 = jnp.bfloat16
f32 = jnp.float32


def dot_nn(a, b):
    return lax.dot_general(a, b, (((1,), (0,)), ((), ())), preferred_element_type=f32)


def dot_nt(a, b):
    return lax.dot_general(a, b, (((1,), (1,)), ((), ())), preferred_element_type=f32)


def one_hot(cond):
    return jnp.where(cond, 1.0, 0.0).astype(bf16)


def iota(shape, dim):
    return lax.broadcasted_iota(jnp.int32, shape, dim)


def adam_refs(param, moment, second, gradient, out_param, out_moment, out_second):
    new_moment = beta_one * moment[...] + (1.0 - beta_one) * gradient
    new_second = beta_two * second[...] + (1.0 - beta_two) * gradient * gradient
    out_moment[...] = new_moment
    out_second[...] = new_second
    out_param[...] = param[...] - learn_rate * (new_moment / bias_one) / (
        jnp.sqrt(new_second / bias_two) + adam_eps
    )


def exchange_kernel(
    tenant_hbm,
    adv_hbm,
    acts_hbm,
    cot_hbm,
    w_hbm,
    ap_hbm,
    am_hbm,
    av_hbm,
    bp_hbm,
    bm_hbm,
    bv_hbm,
    gi_ref,
    ap_out,
    am_out,
    av_out,
    bp_out,
    bm_out,
    bv_out,
    tenant_ref,
    adv_ref,
    xb,
    cot,
    ap,
    am,
    av,
    bp,
    bm,
    bv,
    sx,
    sxe,
    ssm,
    rx,
    rxe,
    rsm,
    rs_all,
    scaled,
    a_all,
    b_all,
    w_all,
    back_s,
    back_t,
    mid_s,
    gbp,
    part,
    sd,
    se,
    rd,
    rde,
    ls_send,
    ls_recv,
    gs_send,
    gs_recv,
    loc_sem,
    a2a_ss,
    a2a_rs,
    ag_ss,
    ag_rs,
    bg_ss,
    bg_rs,
    wg_ss,
    wg_rs,
    wx_ss,
    wx_rs,
    wf_ss,
    wf_rs,
    rs_ss,
    rs_rs,
    gr_ss,
    gr_rs,
):
    me = lax.axis_index("dp")
    z = lax.axis_index("fsdp")
    core = lax.rem(me, 2)
    mate = me + 1 - 2 * core
    x = me // 8
    y = lax.rem(me // 2, 4)
    quarter = lax.rem(x * (1 + core) + y * (2 - core), 4)

    def chip(cx, cy):
        return (lax.rem(cx, 4) * 4 + lax.rem(cy, 4)) * 2 + core

    near = (
        chip(x + 1 - core, y + core),
        chip(x + 3 * (1 - core), y + 3 * core),
        chip(x + core, y + 1 - core),
        chip(x + 3 * core, y + 3 * (1 - core)),
    )
    right = lax.rem(z + 1, NZ)
    left = lax.rem(z + NZ - 1, NZ)
    zside = (right, left)
    zfar = (lax.rem(z + 4, NZ), lax.rem(z + NZ - 4, NZ))

    loads = [
        pltpu.make_async_copy(src, dst, loc_sem.at[i])
        for i, (src, dst) in enumerate(
            [
                (tenant_hbm, tenant_ref),
                (adv_hbm, adv_ref),
                (bp_hbm, bp),
                (ap_hbm, ap),
                (cot_hbm, cot),
                (am_hbm, am),
                (av_hbm, av),
                (bm_hbm, bm),
                (bv_hbm, bv),
                *[
                    (
                        w_hbm.at[(2 * c + k) * WR : (2 * c + k + 1) * WR, :],
                        w_all.at[c, k, 0],
                    )
                    for c in range(4)
                    for k in range(2)
                ],
                *[
                    (
                        acts_hbm.at[:, pl.ds(pl.multiple_of(lax.rem(z + r, NZ) * DB, DB), DB)],
                        xb.at[:, r * DB : r * DB + DB],
                    )
                    for r in range(NZ)
                ],
            ]
        )
    ]
    for load in loads:
        load.start()
    barrier = pltpu.get_barrier_semaphore()

    def greet(k, carry):
        pl.semaphore_signal(
            barrier, inc=1, device_id=(lax.rem(me + k, ND), z), device_id_type=MESH
        )
        return carry

    lax.fori_loop(1, ND, greet, 0)
    for side in (*zside, *zfar):
        pl.semaphore_signal(barrier, inc=1, device_id=(me, side), device_id_type=MESH)

    loads[2].wait()
    b_all[pl.ds(pl.multiple_of(z * BB, BB), BB), :] = (
        bp[...] * ADAPTER_RANK ** (-0.5)
    ).astype(bf16)
    loads[3].wait()
    a_all[0:DB, :] = (
        ap[...] * MODEL_WIDTH ** (-0.5)
    ).astype(bf16)

    loads[0].wait()
    loads[1].wait()
    t_row = tenant_ref[...]
    t_col = jnp.broadcast_to(t_row.astype(f32), (RD, RD)).T.astype(jnp.int32)
    adv_col = jnp.broadcast_to(adv_ref[...].astype(f32), (RD, RD)).T[:, 0:1]
    o_row = jnp.right_shift(t_row, 3)
    o_col = jnp.right_shift(t_col, 3)
    tl = jnp.bitwise_and(t_col, TEN_DEV - 1).astype(f32).astype(bf16)
    same = o_col == o_row
    earlier_rows = jnp.where(same & (iota((RD, RD), 0) < iota((RD, RD), 1)), 1.0, 0.0)
    rank_row = jnp.sum(earlier_rows, axis=0, keepdims=True).astype(jnp.int32)
    earlier_cols = jnp.where(same & (iota((RD, RD), 1) < iota((RD, RD), 0)), 1.0, 0.0)
    rank_col = jnp.sum(earlier_cols, axis=1, keepdims=True).astype(jnp.int32)
    key8_row = jnp.where(rank_row < SB, o_row * SB + rank_row, -1)
    key9_row = jnp.where(rank_row == SB, o_row, -1)
    o_col1 = o_col[:, 0:1]
    key8_col = jnp.where(rank_col < SB, o_col1 * SB + rank_col, -1)
    key9_col = jnp.where(rank_col == SB, o_col1, -1)
    p8 = one_hot(iota((MR, RD), 0) == key8_row)
    ext_rows = jnp.right_shift(iota((MR, RD), 0), 3) == key9_row
    ext_piece = jnp.bitwise_and(iota((MR, RD), 0), PC - 1)

    def pack9(p):
        return one_hot(ext_rows & (ext_piece == p))

    pl.semaphore_wait(barrier, ND - 1 + 4)

    def a2a_start(src, dst, c0, cw, i):
        def go(k, carry):
            peer = lax.rem(me + k, ND)
            pltpu.make_async_remote_copy(
                src_ref=src.at[pl.ds(pl.multiple_of(peer * SB, SB), SB), pl.ds(c0, cw)],
                dst_ref=dst.at[pl.ds(pl.multiple_of(me * SB, SB), SB), pl.ds(c0, cw)],
                send_sem=a2a_ss.at[i],
                recv_sem=a2a_rs.at[i],
                device_id=(peer, z),
                device_id_type=MESH,
            ).start()
            return carry

        lax.fori_loop(1, ND, go, 0)
        own = pl.ds(pl.multiple_of(me * SB, SB), SB)
        dst[own, c0 : c0 + cw] = src[own, c0 : c0 + cw]

    def a2a_all(src, dst, c0, cw, i):
        return pltpu.make_async_remote_copy(
            src_ref=src.at[pl.ds(0, MR - SB), pl.ds(c0, cw)],
            dst_ref=dst.at[pl.ds(0, MR - SB), pl.ds(c0, cw)],
            send_sem=a2a_ss.at[i],
            recv_sem=a2a_rs.at[i],
            device_id=(mate, z),
            device_id_type=MESH,
        )

    steps = (NZ // 2, NZ // 2 - 1)
    HB = DB // 2

    def a_copy(dr, s, q):
        src, dst = ((NZ - s) % NZ, NZ - 1 - s) if dr == 0 else (s, s + 1)
        return pltpu.make_async_remote_copy(
            src_ref=a_all.at[pl.ds(src * DB + q * HB, HB), :],
            dst_ref=a_all.at[pl.ds(dst * DB + q * HB, HB), :],
            send_sem=ag_ss.at[dr, s, q],
            recv_sem=ag_rs.at[dr, s, q],
            device_id=(me, zside[dr]),
            device_id_type=MESH,
        )

    def b_copy(dr, dist):
        block = lax.rem(z + (NZ - dist % 8 if dr == 0 else dist % 8), NZ)
        view = b_all.at[pl.ds(pl.multiple_of(block * BB, BB), BB), :]
        return pltpu.make_async_remote_copy(
            src_ref=view,
            dst_ref=view,
            send_sem=bg_ss.at[dr, dist],
            recv_sem=bg_rs.at[dr, dist],
            device_id=(me, zfar[dr] if dist == 8 else zside[dr]),
            device_id_type=MESH,
        )

    b_plan = (
        ((), (0, 8)),
        ((0, 8), (1, 4)),
        ((1, 4), (2, 5)),
        ((2, 5), (6,)),
        ((6,), (7,)),
        ((7,), ()),
    )
    b_sent = ((0, 8, 1, 4, 2, 5, 6, 7), (0, 8, 1, 4, 2, 5, 6))

    def w_copy(dr, s):
        src, dst = ((NZ - s) % NZ, NZ - 1 - s) if dr == 0 else (s, s + 1)
        return pltpu.make_async_remote_copy(
            src_ref=w_all.at[quarter, core, src],
            dst_ref=w_all.at[quarter, core, dst],
            send_sem=wg_ss.at[dr, s],
            recv_sem=wg_rs.at[dr, s],
            device_id=(me, zside[dr]),
            device_id_type=MESH,
        )

    def w_span(i, t):
        first, count = W_RANGES[i]
        half = (count + 1) // 2
        return ((first, count), (first, count), (first, half), (first + half, count - half))[t]

    def w_near(i, t):
        first, count = w_span(i, t) if t < 4 else W_RANGES[i]
        view = w_all.at[quarter, core, pl.ds(first, count)]
        return pltpu.make_async_remote_copy(
            src_ref=view,
            dst_ref=view,
            send_sem=wx_ss.at[t, i],
            recv_sem=wx_rs.at[t, i],
            device_id=(near[t] if t < 4 else mate, z),
            device_id_type=MESH,
        )

    def w_mate(i, t):
        first, count = w_span(i, t)
        view = w_all.at[
            lax.rem(quarter + (3, 1, 2, 2)[t], 4), core, pl.ds(first, count)
        ]
        return pltpu.make_async_remote_copy(
            src_ref=view,
            dst_ref=view,
            send_sem=wf_ss.at[t, i],
            recv_sem=wf_rs.at[t, i],
            device_id=(mate, z),
            device_id_type=MESH,
        )

    def w_spread(i):
        for t in range(5):
            w_near(i, t).start()

    def w_forward(i):
        for t in range(4):
            w_near(i, t).wait_recv()
            w_mate(i, t).start()

    def base_block(slot):
        block = lax.rem(z + slot, NZ)
        cols = pl.ds(pl.multiple_of(block * DB, DB), DB)
        rows = jnp.concatenate(
            [w_all[c, k, slot] for c in range(4) for k in range(2)], axis=0
        )
        gi_ref[:, cols] = dot_nt(scaled[...], rows).astype(bf16)

    def base_range(i):
        w_near(i, 4).wait_recv()
        for t in range(4):
            w_mate(i, t).wait_recv()
        first, count = W_RANGES[i]
        for slot in range(first, first + count):
            base_block(slot)

    def ab_step(s):
        if s < len(b_plan):
            for dr in (0, 1):
                for dist in b_plan[s][0]:
                    if dist in b_sent[dr]:
                        b_copy(dr, dist).wait_recv()
                for dist in b_plan[s][1]:
                    if dist in b_sent[dr]:
                        b_copy(dr, dist).start()
        for q in (0, 1):
            for dr in (0, 1):
                if s > 0 and s - 1 < steps[dr]:
                    a_copy(dr, s - 1, q).wait_recv()
                if s < steps[dr]:
                    a_copy(dr, s, q).start()
        for dr in (0, 1):
            if s > 0 and s - 1 < steps[dr]:
                w_copy(dr, s - 1).wait_recv()
            if s < steps[dr]:
                w_copy(dr, s).start()

    down_coefficient = adapter_scale * MODEL_WIDTH ** (-0.5)
    up_coefficient = adapter_scale * ADAPTER_RANK ** (-0.5)

    rsteps = (NZ // 2, NZ // 2 - 1)

    def a_partial(slot):
        return down_coefficient * dot_nn(back_t[...], rx[:, slot * DB : slot * DB + DB])

    def rs_copy(dr, k, q):
        rows = pl.ds(q * HB, HB)
        return pltpu.make_async_remote_copy(
            src_ref=ls_send.at[dr, k, rows, :],
            dst_ref=ls_recv.at[dr, k, rows, :],
            send_sem=rs_ss.at[dr, k, q],
            recv_sem=rs_rs.at[dr, k, q],
            device_id=(me, (left, right)[dr]),
            device_id_type=MESH,
        )

    def rs_parts(k):
        for dr in (0, 1):
            if k < rsteps[dr]:
                part[dr] = a_partial(8 + k if dr == 0 else 7 - k)

    def rs_step(k):
        for q in (0, 1):
            rows = slice(q * HB, q * HB + HB)
            for dr in (0, 1):
                if k < rsteps[dr]:
                    total = part[dr, rows, :]
                    if k > 0:
                        rs_copy(dr, k - 1, q).wait_recv()
                        total = total + ls_recv[dr, k - 1, rows, :].astype(f32)
                    ls_send[dr, k, rows, :] = total.astype(bf16)
                    rs_copy(dr, k, q).start()

    def gb_rows(slot):
        block = lax.rem(z + slot, NZ)
        return gbp[pl.ds(pl.multiple_of(block * BB, BB), BB), :]

    def gb_copy(dr, dist):
        return pltpu.make_async_remote_copy(
            src_ref=gs_send.at[dr, dist - 1],
            dst_ref=gs_recv.at[dr, dist - 1],
            send_sem=gr_ss.at[dr, dist - 1],
            recv_sem=gr_rs.at[dr, dist - 1],
            device_id=(me, (zfar[1 - dr] if dist == 4 else (left, right)[dr])),
            device_id_type=MESH,
        )

    def gb_send(dr, dist):
        total = gb_rows(NZ - dist if dr == 0 else dist)
        if dist not in (3, 8 if dr == 0 else 7):
            gb_copy(dr, dist + 1).wait_recv()
            total = total + gs_recv[dr, dist].astype(f32)
        gs_send[dr, dist - 1] = total.astype(bf16)
        gb_copy(dr, dist).start()

    gb_plan = (((8, 3), (7, 3)), ((7, 2), (6, 2)), ((6, 1), (5, 1)), ((5,), (4,)), ((4,), ()))

    def gb_step(k):
        for dr in (0, 1):
            for dist in gb_plan[k][dr]:
                gb_send(dr, dist)

    def put9(p):
        return one_hot(iota((MR, ND), 0) == iota((MR, ND), 1) * PC + p)

    def side_pair(p, acc):
        term = (
            adapter_scale * dot_nt(back_s[...], a_all[p * PW : p * PW + PW, :])
        ).astype(bf16)
        sd[:, p * PW : p * PW + PW] = term[0:MR]
        a2a_start(sd, rd, p * PW, PW, 10 + p)
        return acc + dot_nn(put9(p), term[MR:AR])

    def pick9(p):
        return one_hot(iota((ND, MR), 1) == iota((ND, MR), 0) * PC + p)

    def acts_pair(p):
        sx[:, p * PW : p * PW + PW] = dot_nn(p8, xb[:, p * PW : p * PW + PW]).astype(bf16)
        a2a_start(sx, rx, p * PW, PW, 2 + p)

    def acts_wait(*pairs):
        for p in pairs:
            a2a_all(sx, rx, p * PW, PW, 2 + p).wait_recv()

    for i in range(9, 17):
        loads[i].wait()
    ab_step(0)
    loads[4].wait()
    scaled_rows = (cot[...].astype(f32) * (adv_col * 0.25)).astype(bf16)
    scaled[...] = scaled_rows
    ssm[:, 0:KF] = dot_nn(p8, scaled_rows).astype(bf16)
    ssm[:, KF : KF + 128] = dot_nn(p8, tl).astype(bf16)
    misc = jnp.zeros((MR, 128), f32)
    for p in range(PC):
        part9 = scaled_rows[:, 128 * p : 128 * p + 128] if p < 4 else tl
        misc = misc + dot_nn(pack9(p), part9)
    ssm[:, KF + 128 : KF + 256] = misc.astype(bf16)

    a2a_start(ssm, rsm, 0, SMW, 0)
    for i in range(17, 17 + NZ):
        loads[i].wait()

    def pack_pieces(p, acc):
        cols = pl.ds(pl.multiple_of(p * PW, PW), PW)
        return acc + dot_nn(one_hot(ext_rows & (ext_piece == p)), xb[:, cols])

    sxe[...] = lax.fori_loop(0, PC, pack_pieces, jnp.zeros((MR, PW), f32)).astype(bf16)
    a2a_start(sxe, rxe, 0, PW, 1)
    acts_pair(3)
    acts_pair(4)
    ab_step(1)
    acts_pair(5)
    acts_pair(2)
    acts_pair(6)
    acts_pair(1)
    ab_step(2)
    acts_pair(7)
    acts_pair(0)

    a2a_all(ssm, rsm, 0, SMW, 0).wait_recv()
    rs_all[0:MR, :] = rsm[:, 0:KF]
    misc_in = rsm[:, KF + 128 : KF + 256]
    for p in range(4):
        rs_all[MR:AR, 128 * p : 128 * p + 128] = dot_nn(pick9(p), misc_in).astype(bf16)
    t_all = jnp.concatenate(
        [rsm[:, KF : KF + 128].astype(f32), dot_nn(pick9(4), misc_in)], axis=0
    ).astype(jnp.int32)
    mask = jnp.right_shift(iota((AR, CB), 1), 5) == jnp.concatenate([t_all, t_all], axis=1)
    ab_step(3)
    base_block(0)
    ab_step(4)
    w_spread(0)
    w_spread(1)
    ab_step(5)
    back_f = jnp.where(mask, dot_nt(rs_all[...], b_all[...]), 0.0)
    back_s[...] = back_f.astype(bf16)
    back_t[...] = back_f.T.astype(bf16)
    ext = side_pair(0, jnp.zeros((MR, PW), f32))
    a2a_all(sxe, rxe, 0, PW, 1).wait_recv()
    for p in range(PC):
        rx[MR:AR, p * PW : p * PW + PW] = dot_nn(pick9(p), rxe[...]).astype(bf16)
    acts_wait(3, 4)
    rs_parts(0)
    rs_step(0)
    ext = side_pair(7, ext)
    ab_step(6)
    rs_parts(1)
    rs_step(1)
    ext = side_pair(1, ext)
    ext = side_pair(6, ext)
    ab_step(7)
    acts_wait(5, 2)
    rs_parts(2)
    rs_step(2)
    ext = side_pair(2, ext)
    ext = side_pair(5, ext)
    ab_step(8)
    rs_parts(3)
    rs_step(3)
    ext = side_pair(3, ext)
    ext = side_pair(4, ext)
    se[...] = ext.astype(bf16)
    a2a_start(se, rde, 0, PW, 18)
    w_spread(2)
    w_spread(3)
    acts_wait(6, 1)
    rs_parts(4)
    acts_wait(7, 0)
    mid = dot_nn(rx[...], a_all[...])
    mid_s[...] = jnp.where(mask, mid, 0.0).T.astype(bf16)
    gbp[...] = up_coefficient * dot_nn(mid_s[...], rs_all[...])
    gb_step(0)
    rs_step(4)
    rs_parts(5)
    gb_step(1)
    rs_step(5)
    rs_parts(6)
    w_forward(0)
    w_forward(1)
    gb_step(2)
    rs_step(6)
    rs_parts(7)
    gb_step(3)
    rs_step(7)
    gb_step(4)
    base_range(0)
    base_range(1)
    w_forward(2)
    w_forward(3)
    base_range(2)
    base_range(3)
    total = a_partial(0)
    for q in (0, 1):
        for dr in (0, 1):
            rs_copy(dr, rsteps[dr] - 1, q).wait_recv()
    total = total + ls_recv[0, rsteps[0] - 1].astype(f32)
    total = total + ls_recv[1, rsteps[1] - 1].astype(f32)
    for i in range(5, 9):
        loads[i].wait()
    adam_refs(ap, am, av, total.T, ap_out, am_out, av_out)
    total_b = gb_rows(0)
    for dr in (0, 1):
        for dist in (1, 4):
            gb_copy(dr, dist).wait_recv()
            total_b = total_b + gs_recv[dr, dist - 1].astype(f32)
    adam_refs(bp, bm, bv, total_b, bp_out, bm_out, bv_out)

    r8 = one_hot(iota((RD, MR), 1) == key8_col)
    back_rows = jnp.right_shift(iota((RD, MR), 1), 3) == key9_col
    back_piece = jnp.bitwise_and(iota((RD, MR), 1), PC - 1)
    for p in range(PC):
        a2a_all(sd, rd, p * PW, PW, 10 + p).wait_recv()
    a2a_all(se, rde, 0, PW, 18).wait_recv()
    for p in range(PC):
        r9 = one_hot(back_rows & (back_piece == p))
        side_rows = dot_nn(r8, rd[:, p * PW : p * PW + PW]) + dot_nn(r9, rde[...])
        side_rows = side_rows.astype(bf16).astype(f32)
        for h in (0, 1):
            block = lax.rem(z + 2 * p + h, NZ)
            cols = pl.ds(pl.multiple_of(block * DB, DB), DB)
            gi_ref[:, cols] = (
                gi_ref[:, cols].astype(f32) + side_rows[:, h * DB : h * DB + DB]
            ).astype(bf16)

    a2a_all(ssm, rsm, 0, SMW, 0).wait_send()
    for p in range(PC):
        a2a_all(sx, rx, p * PW, PW, 2 + p).wait_send()
        a2a_all(sd, rd, p * PW, PW, 10 + p).wait_send()
    a2a_all(sxe, rxe, 0, PW, 1).wait_send()
    a2a_all(se, rde, 0, PW, 18).wait_send()
    for i in range(len(W_RANGES)):
        for t in range(5):
            w_near(i, t).wait_send()
        for t in range(4):
            w_mate(i, t).wait_send()
    for dr in (0, 1):
        for s in range(steps[dr]):
            for q in (0, 1):
                a_copy(dr, s, q).wait_send()
            w_copy(dr, s).wait_send()
        for k in range(rsteps[dr]):
            for q in (0, 1):
                rs_copy(dr, k, q).wait_send()
            gb_copy(dr, k + 1).wait_send()
        for dist in b_sent[dr]:
            b_copy(dr, dist).wait_send()


def finish_kernel(*refs):
    n = len(refs) // 2
    sems = refs[-1]
    copies = [pltpu.make_async_copy(refs[i], refs[n + i], sems.at[i]) for i in range(n)]
    for copy in copies:
        copy.start()
    for copy in copies:
        copy.wait()


def per_device(
    acts,
    cotangent,
    tenant,
    advantage,
    base_weight,
    a_param,
    a_moment,
    a_second,
    b_param,
    b_moment,
    b_second,
):
    vmem = pl.BlockSpec(memory_space=pltpu.VMEM)
    hbm = pl.BlockSpec(memory_space=pltpu.HBM)
    dma = pltpu.SemaphoreType.DMA
    v = pltpu.VMEM
    out_shape = (
        jax.ShapeDtypeStruct((RD, D), bf16),
        *[jax.ShapeDtypeStruct((DB, CB), f32)] * 3,
        *[jax.ShapeDtypeStruct((BB, KF), f32)] * 3,
    )
    results = pl.pallas_call(
        exchange_kernel,
        out_shape=out_shape,
        in_specs=[hbm] * 11,
        out_specs=(vmem,) * 7,
        scratch_shapes=[
            v((1, RD), jnp.int32),
            v((1, RD), jnp.int32),
            v((RD, D), bf16),
            v((RD, KF), bf16),
            v((DB, CB), f32),
            v((DB, CB), f32),
            v((DB, CB), f32),
            v((BB, KF), f32),
            v((BB, KF), f32),
            v((BB, KF), f32),
            v((MR, D), bf16),
            v((MR, PW), bf16),
            v((MR, SMW), bf16),
            v((AR, D), bf16),
            v((MR, PW), bf16),
            v((MR, SMW), bf16),
            v((AR, KF), bf16),
            v((RD, KF), bf16),
            v((D, CB), bf16),
            v((CB, KF), bf16),
            v((4, 2, NZ, WR, KF), bf16),
            v((AR, CB), bf16),
            v((CB, AR), bf16),
            v((CB, AR), bf16),
            v((CB, KF), f32),
            v((2, CB, DB), f32),
            v((MR, D), bf16),
            v((MR, PW), bf16),
            v((MR, D), bf16),
            v((MR, PW), bf16),
            v((2, 8, CB, DB), bf16),
            v((2, 8, CB, DB), bf16),
            v((2, 8, BB, KF), bf16),
            v((2, 8, BB, KF), bf16),
            dma((17 + NZ,)),
            dma((19,)),
            dma((19,)),
            dma((2, 8, 2)),
            dma((2, 8, 2)),
            dma((2, 9)),
            dma((2, 9)),
            dma((2, 8)),
            dma((2, 8)),
            dma((5, 4)),
            dma((5, 4)),
            dma((4, 4)),
            dma((4, 4)),
            dma((2, 8, 2)),
            dma((2, 8, 2)),
            dma((2, 8)),
            dma((2, 8)),
        ],
        compiler_params=pltpu.CompilerParams(
            collective_id=0, has_side_effects=True, vmem_limit_bytes=48 * 1024 * 1024
        ),
        name="exchange",
    )(
        *[
            pltpu.with_memory_space_constraint(x, pltpu.HBM)
            for x in (
                tenant.reshape(1, RD),
                advantage.reshape(1, RD),
                acts,
                cotangent,
                base_weight,
                a_param,
                a_moment,
                a_second,
                b_param,
                b_moment,
                b_second,
            )
        ]
    )
    return tuple(
        pl.pallas_call(
            finish_kernel,
            out_shape=out_shape,
            in_specs=[vmem] * 7,
            out_specs=(hbm,) * 7,
            scratch_shapes=[dma((7,))],
            compiler_params=pltpu.CompilerParams(vmem_limit_bytes=1024 * 1024),
            name="finish",
        )(*results)
    )


def solution(mesh):
    in_specs = (
        P(("dp", "fsdp"), None),
        P(("dp", "fsdp"), None),
        P(("dp", "fsdp")),
        P(("dp", "fsdp")),
        P("fsdp", None),
        P("fsdp", "dp"),
        P("fsdp", "dp"),
        P("fsdp", "dp"),
        P(("dp", "fsdp"), None),
        P(("dp", "fsdp"), None),
        P(("dp", "fsdp"), None),
    )
    out_specs = (
        P(("dp", "fsdp"), None),
        P("fsdp", "dp"),
        P("fsdp", "dp"),
        P("fsdp", "dp"),
        P(("dp", "fsdp"), None),
        P(("dp", "fsdp"), None),
        P(("dp", "fsdp"), None),
    )
    return jax.shard_map(
        per_device, mesh=mesh, in_specs=in_specs, out_specs=out_specs, check_vma=False
    )
```
